32 devices in a mesh: row: 4 (over x, core), col: 8 (over z, y).
Axes of the slice: x: 2, y: 2, z: 4, core: 2. Of those that a mesh axis runs over, the one named last changes fastest.
Arguments:
- trailing: float32 [4096, 4096], P('row', 'col'), may hold values from -6 to 6
- panel_left: float32 [4096, 384], P(('row', 'col')), may hold values from -0.3125 to 0.3125
- panel_right: float32 [8, 1024, 384], P('row', 'col'), may hold values from -1 to 1
- panel_solved: float32 [1024, 1024], P('row', 'col'), may hold values from -1.75 to 1.75
- right_sides: float32 [4096, 1024], P('row', 'col'), may hold values from -6 to 6
- tile_ranks: int32 [8], replicated, may hold values from 64 to 384, as said below
- tile_order: int32 [8], replicated, may hold values from 0 to 7, each once
Outputs:
- trail_new: float32 [4096, 4096], P('row', 'col')
- rhs_new: float32 [4096, 1024], P('row', 'col')
The draws below stay inside these ranges and needn't reach their ends.
Inputs may be any that keep to these rules, and one draw needn't show every extreme that they name: `tile_ranks`: every rank is a multiple of 64; both 64 and 384 occur in every draw. `tile_order`: each tile appears in exactly one slot.
All inputs are finite; a program needn't handle non-finite values.
Results may differ from the reference program's by a relative error of at most 0.00008.
Values sent between devices are 32-bit elements; how exact they have to be, the bound alone decides.
A program may use at most 64 MiB of HBM per device.

```python
import jax
import jax.numpy as jnp
from jax import lax

TILE = 512
PANEL = 1024
RSTEP = 64
RMAX = 384
TILES = 8
ORDER = 4096
RHS_COLS = 1024


def draw_tile_ranks(key, part):
    first_key, second_key = jax.random.split(jax.random.fold_in(key, 17))
    levels = jax.random.randint(first_key, (TILES,), 1, 7)
    spots = jax.random.permutation(second_key, TILES)
    places = jnp.arange(TILES)
    levels = jnp.where(places == spots[0], 6, levels)
    levels = jnp.where(places == spots[1], 1, levels)
    return (levels * RSTEP).astype(jnp.int32)


def level_of(key, extent, cuts, least, high):
    loudness = 1.0
    for position, shards_of in cuts:
        draws = jax.random.uniform(jax.random.fold_in(jax.random.fold_in(key, 6), position), (shards_of,), jnp.float32, least / len(cuts), high / len(cuts))
        loudness = loudness * jnp.repeat(jnp.exp(draws), extent[position] // shards_of).reshape((-1,) + (1,) * (len(extent) - 1 - position))
    return loudness


def gaussian(rng, shape, spread, limit, cuts=(), kind=jnp.bfloat16):
    array = jax.random.normal(rng, shape, jnp.float32) * spread
    if len(cuts) > 0:
        array = level_of(rng, shape, cuts, -0.22, 0.18) * array
    return jnp.clip(array, min=-limit, max=limit).astype(kind)


def setup_inputs(seed: int = 0) -> dict:
    key_list = jax.random.split(jax.random.key(seed), 8)
    trailing = gaussian(key_list[0], (ORDER, ORDER), 1.0, 6.0, ((0, 4), (1, 8)), jnp.float32)
    panel_left = gaussian(key_list[1], (ORDER, RMAX), RMAX ** -0.5, 0.3125, ((0, 32),), jnp.float32)
    panel_right = gaussian(key_list[2], (TILES, PANEL, RMAX), (PANEL ** -0.25), 1.0, ((0, 4), (1, 8)), jnp.float32)
    panel_solved = gaussian(key_list[3], (PANEL, RHS_COLS), 0.3, 1.75, ((0, 4), (1, 8)), jnp.float32)
    right_sides = gaussian(key_list[4], (ORDER, RHS_COLS), 1.0, 6.0, ((0, 4), (1, 8)), jnp.float32)
    tile_ranks = draw_tile_ranks(jax.random.fold_in(key_list[7], 71), 0)
    tile_order = jax.random.permutation(key_list[6], TILES).astype(jnp.int32)
    return {"trailing": trailing, "panel_left": panel_left, "panel_right": panel_right, "panel_solved": panel_solved, "right_sides": right_sides, "tile_ranks": tile_ranks, "tile_order": tile_order}


def reference(trailing, panel_left, panel_right, panel_solved, right_sides, tile_ranks, tile_order):
    places = jnp.arange(TILES, dtype=jnp.int32)
    slot_rank = jnp.take(tile_ranks, tile_order)
    keep_mask = (jnp.arange(RMAX, dtype=jnp.int32)[None, :] < slot_rank[:, None]).astype(jnp.float32)
    left_factor = panel_left.reshape(TILES, TILE, RMAX) * keep_mask[:, None, :]
    panel_l = jnp.einsum("sik,sjk->sij", left_factor, panel_right, precision=lax.Precision.HIGHEST).reshape(TILES * TILE, PANEL)
    slot_of = jnp.zeros((TILES,), jnp.int32).at[tile_order].set(places)
    column_l = jnp.take(panel_l.reshape(TILES, TILE, PANEL), slot_of, axis=0).reshape(TILES * TILE, PANEL)
    trail_new = trailing - jnp.dot(panel_l, column_l.T, precision=lax.Precision.HIGHEST, preferred_element_type=jnp.float32)
    rhs_new = right_sides - jnp.dot(panel_l, panel_solved, precision=lax.Precision.HIGHEST, preferred_element_type=jnp.float32)
    return trail_new, rhs_new
```

```python
import functools

import jax
import jax.numpy as jnp
from jax import lax
from jax.experimental import pallas as pl
from jax.experimental.pallas import tpu as pltpu
from jax.sharding import PartitionSpec as P

MESH = pl.DeviceIdType.MESH
ACROSS = 2
CORES = 2
GATHER_VMEM = 30 * 1024 * 1024
UPDATE_VMEM = 16 * 1024 * 1024


def find(order, value):
    place = jnp.int32(0)
    for i in range(order.shape[0]):
        place = jnp.where(order[i] == value, jnp.int32(i), place)
    return place


def chain(where, root_row, root_team, candidate, tile_at, first_out, first_in, chip, far_in, fs, fr, xs, xr, ts, tr):
    row, col, team, core, teams = where
    pair = team * CORES + (1 - core)

    def f_copy(u):
        return pltpu.make_async_remote_copy(first_out.at[u], first_in.at[u], fs.at[u], fr.at[u], device_id=(pair, col), device_id_type=MESH)

    def x_copy(u, k, source):
        to = lax.rem(team + k, teams)
        return pltpu.make_async_remote_copy(chip.at[u], far_in.at[source, u], xs.at[k, u], xr.at[source, u], device_id=(to * CORES + core, col), device_id_type=MESH)

    def t_copy(u, which):
        ref = tile_at(u, which)
        return pltpu.make_async_remote_copy(ref, ref, ts.at[u], tr.at[u], device_id=(pair, col), device_id_type=MESH)

    def one(u):
        first_out[u] = candidate(u, 1 - core)
        f_copy(u).start()

    def two(u):
        mine = candidate(u, core)
        f_copy(u).wait_recv()
        chip[u] = jnp.where(root_row == row, mine, first_in[u])
        for k in range(1, teams):
            x_copy(u, k, team).start()

    def three(u):
        value = chip[u]
        for k in range(1, teams):
            other = lax.rem(team + k, teams)
            x_copy(u, k, other).wait_recv()
            value = jnp.where(root_team == other, far_in[other, u], value)
        tile_at(u, core)[...] = value
        t_copy(u, core).start()

    def ready(u):
        t_copy(u, 1 - core).wait_recv()

    def drain(u):
        f_copy(u).wait_send()
        for k in range(1, teams):
            x_copy(u, k, team).wait_send()
        t_copy(u, core).wait_send()

    return one, two, three, ready, drain


def gather_kernel(n_row, n_col, slots, order, ranks, left, right, solved, trailing, sides_in, a_high, a_low, a_rest, tile_l, trail_here, sides_here,
                  rows_l, rows_r, tile_r, rows_w, both, mid_high, mid_low, rf_out, rf_in, r_chip, r_far, lf_out, lf_in, l_chip, l_far,
                  own_sem, held_sem, rsem, zsem, ysem, wsem, wrsem, rfs, rfr, rxs, rxr, rts, rtr, lfs, lfr, lxs, lxr, lts, ltr):
    length = n_col // ACROSS
    half = length // slots
    teams = n_row // CORES
    depth, width = rows_r.shape[2], rows_r.shape[3]
    cut = left.shape[0] // 2
    early, late = slots, slots + 1
    row, col = lax.axis_index("row"), lax.axis_index("col")
    z, y = col // ACROSS, col % ACROSS
    team, core = row // CORES, row % CORES
    mate = z * ACROSS + (1 - y)
    last_up, last_down = z, length - 1 - z
    most = jnp.maximum(last_up, last_down)
    through = ((z > 0) & (z < length - 1)).astype(jnp.int32)

    barrier = pltpu.get_barrier_semaphore()

    def greet(r, c):
        pl.semaphore_signal(barrier, inc=1, device_id=(r, c), device_id_type=MESH)

    @pl.when(z > 0)
    def _():
        greet(row, col - ACROSS)

    @pl.when(z < length - 1)
    def _():
        greet(row, col + ACROSS)

    greet(row, mate)
    for k in range(1, n_row):
        greet(lax.rem(row + k, n_row), col)

    def w_rows(r):
        size = solved.shape[0]
        return rows_w.at[pl.ds(pl.multiple_of(r * size, size), size)]

    own = [pltpu.make_async_copy(right.at[s], rows_r.at[s, col], own_sem.at[s]) for s in range(slots)]
    own.append(pltpu.make_async_copy(left, rows_l.at[col], own_sem.at[slots]))
    own.append(pltpu.make_async_copy(solved, w_rows(row), own_sem.at[slots + 1]))
    for copy in own:
        copy.start()
    pl.semaphore_wait(barrier, (z > 0).astype(jnp.int32) + (z < length - 1).astype(jnp.int32) + n_row)

    def piece(p, c):
        if p == early:
            return rows_l.at[c, pl.ds(0, cut)]
        if p == late:
            return rows_l.at[c, pl.ds(cut, cut)]
        return rows_r.at[p, c]

    def mine(p):
        if p == early:
            return left.at[pl.ds(0, cut)]
        if p == late:
            return left.at[pl.ds(cut, cut)]
        return right.at[p]

    def z_copy(p, src, way, across=False, fresh=False):
        c = src * ACROSS + ((1 - y) if across else y)
        lane = late + 1 if across else p
        to = col + (ACROSS if way == 0 else -ACROSS)
        return pltpu.make_async_remote_copy(mine(p) if fresh else piece(p, c), piece(p, c), zsem.at[way, lane, src], rsem.at[p, c], device_id=(row, to), device_id_type=MESH)

    def y_copy(p, src, c, fresh=False):
        return pltpu.make_async_remote_copy(mine(p) if fresh else piece(p, c), piece(p, c), ysem.at[p, src], rsem.at[p, c], device_id=(row, mate), device_id_type=MESH)

    def w_copy(k):
        return pltpu.make_async_remote_copy(solved, w_rows(row), wsem.at[k], wrsem.at[row], device_id=(lax.rem(row + k, n_row), col), device_id_type=MESH)

    def upward(act):
        pl.when(z < length - 1)(functools.partial(act, 0))

    def downward(act):
        pl.when(z > 0)(functools.partial(act, 1))

    def along(side, act):
        (upward if side == 0 else downward)(act)

    def sources(d, body):
        for side in range(2):
            src = z - d if side == 0 else z + d
            ok = (src >= 0) if side == 0 else (src < length)
            pl.when(ok & (d > 0))(functools.partial(body, src, side))

    def near(d, body):
        @pl.when(d == 0)
        def _():
            body(col)

        sources(d, lambda src, side: body(src * ACROSS + y))

    def far(d, body):
        @pl.when(d == 0)
        def _():
            body(mate)

        sources(d, lambda src, side: body(src * ACROSS + 1 - y))

    root_slot = find(order, col)
    local = lax.rem(root_slot, slots)
    root_row = root_slot // slots
    root_team = root_row // CORES
    where = (row, col, team, core, teams)

    def pick(parts):
        value = parts[0]
        for s in range(1, slots):
            value = jnp.where(local == s, parts[s], value)
        return value

    part = depth // CORES

    def rows_of(which):
        return pl.ds(pl.multiple_of(which * part, part), part)

    def r_candidate(c, which):
        return pick([rows_r[s, c, rows_of(which)] for s in range(slots)])

    r_one, r_two, r_three, r_ready, r_drain = chain(
        where, root_row, root_team, r_candidate, lambda c, which: tile_r.at[c, rows_of(which)],
        rf_out, rf_in, r_chip, r_far, rfs, rfr, rxs, rxr, rts, rtr)

    lpart = cut // CORES

    def l_rows(u, which):
        return pl.ds(pl.multiple_of((u % 2) * cut + which * lpart, lpart), lpart)

    def l_candidate(u, which):
        return pick([rows_l[u // 2 + s * half * ACROSS, l_rows(u, which)] for s in range(slots)])

    l_one, l_two, l_three, l_ready, l_drain = chain(
        where, root_row, root_team, l_candidate, lambda u, which: tile_l.at[u // 2, l_rows(u, which)],
        lf_out, lf_in, l_chip, l_far, lfs, lfr, lxs, lxr, lts, ltr)

    def lefts(d, across, which, body):
        def one(q, _):
            last = jnp.abs(z - q)
            for s in range(1, slots):
                last = jnp.maximum(last, jnp.abs(z - q - s * half))

            @pl.when(last == d)
            def _():
                body((q * ACROSS + ((1 - y) if across else y)) * 2 + which)

            return 0

        lax.fori_loop(0, half, one, 0)

    def arrived(p, c):
        ref = piece(p, c)
        pltpu.make_async_remote_copy(ref, ref, ysem.at[p, 0], rsem.at[p, c], device_id=(row, mate), device_id_type=MESH).wait_recv()

    for s in range(slots):
        upward(lambda way: z_copy(s, z, way, fresh=True).start())
        downward(lambda way: z_copy(s, z, way, fresh=True).start())
        y_copy(s, z, col, fresh=True).start()
    y_copy(late, z, col, fresh=True).start()
    for k in range(1, n_row):
        w_copy(k).start()

    def send_left(way):
        z_copy(early, z, way, fresh=True).start()
        z_copy(late, z, way, fresh=True).start()

    @pl.when((last_up == 0) & (z < length - 1))
    def _():
        send_left(0)

    @pl.when((last_down == 0) & (z > 0))
    def _():
        send_left(1)

    both[...] = jnp.zeros_like(both)
    for copy in own:
        copy.wait()
    r_one(col)
    r_two(col)

    held = [pltpu.make_async_copy(trailing, trail_here, held_sem.at[0]), pltpu.make_async_copy(sides_in, sides_here, held_sem.at[1])]
    for copy in held:
        copy.start()

    def relay_rights(t):
        for s in range(slots):
            def one(src, side, s=s):
                arrived(s, src * ACROSS + y)
                along(side, lambda way: z_copy(s, src, way).start())
                y_copy(s, src, src * ACROSS + y).start()

            sources(t, one)

    def own_lefts(t):
        @pl.when((t == last_up) & (z < length - 1))
        def _():
            send_left(0)

        @pl.when((t == last_down) & (z > 0))
        def _():
            send_left(1)

        @pl.when(t == 2)
        def _():
            arrived(late, mate)

        @pl.when((t == jnp.maximum(last_up, 2)) & (z < length - 1))
        def _():
            z_copy(late, z, 0, True).start()

        @pl.when((t == jnp.maximum(last_down, 2)) & (z > 0))
        def _():
            z_copy(late, z, 1, True).start()

        @pl.when(t == most)
        def _():
            y_copy(early, z, col, fresh=True).start()

    def left_arrives(k, d):
        def one(src, side):
            if k == 0:
                arrived(early, src * ACROSS + y)
                y_copy(early, src, src * ACROSS + y).start()
                along(side, lambda way: z_copy(early, src, way).start())
            elif k == 1:
                arrived(late, src * ACROSS + y)
                along(side, lambda way: z_copy(late, src, way).start())
            elif k == 2:
                arrived(late, src * ACROSS + 1 - y)
                along(side, lambda way: z_copy(late, src, way, True).start())
            else:
                arrived(early, src * ACROSS + 1 - y)

        if k == 3:
            @pl.when(d == 1)
            def _():
                arrived(early, mate)

        sources(d, one)

    def left_unit(k, d, body):
        lefts(d, k >= 2, 1 if k in (1, 2) else 0, body)

    def w_wait():
        for k in range(1, n_row):
            w_copy(k).wait_send()
            other = lax.rem(row + k, n_row)
            ref = w_rows(other)
            pltpu.make_async_remote_copy(ref, ref, wsem.at[k], wrsem.at[other], device_id=(other, col), device_id_type=MESH).wait_recv()

    def accumulate(d):
        def one(src, _):
            @pl.when(jnp.abs(z - src) == d)
            def _():
                for across in range(ACROSS):
                    r_ready(src * ACROSS + across)
                start = pl.multiple_of(src * (ACROSS * depth), ACROSS * depth)
                column = tile_r[pl.ds(src * ACROSS, ACROSS)].reshape(ACROSS * depth, width)
                column = cut_two(jnp.concatenate([column, rows_w[pl.ds(start, ACROSS * depth)]], axis=1))
                for s in range(slots):
                    rows = cut_two(rows_r[s, pl.ds(src * ACROSS, ACROSS)].reshape(ACROSS * depth, width))
                    both[s] += dot3(rows, column, ((0,), (0,)))

            return 0

        lax.fori_loop(0, length, one, 0)

    def step(t, _):
        d, f = t - most + through, t - most - 1
        relay_rights(t)
        own_lefts(t)
        near(t, r_one)
        left_arrives(0, d)
        left_unit(0, d, l_one)
        near(t - 1, r_three)
        far(t - 2, r_three)
        left_unit(0, d, l_two)
        left_arrives(1, d)
        left_unit(1, d, l_one)

        @pl.when(t == 1)
        def _():
            for s in range(slots):
                arrived(s, mate)

        def one(src, side):
            for s in range(slots):
                arrived(s, src * ACROSS + 1 - y)

        sources(t - 1, one)
        far(t - 1, r_one)
        near(t, r_two)
        left_arrives(3, f)
        left_unit(3, f, l_one)
        far(t - 1, r_two)
        left_unit(1, d, l_two)
        left_unit(3, f, l_two)

        @pl.when(t == 2)
        def _():
            w_wait()

        accumulate(t - 3)
        left_arrives(2, d)
        left_unit(2, d, l_one)
        left_unit(0, d - 1, l_three)
        left_unit(1, d - 1, l_three)
        left_unit(2, d - 1, l_three)
        left_unit(3, f - 1, l_three)
        left_unit(2, d, l_two)
        return 0

    lax.fori_loop(1, 2 * most + 2, step, 0)

    lane = lax.broadcasted_iota(jnp.int32, (width, mid_high.shape[2]), 1)
    sub = lax.broadcasted_iota(jnp.int32, (width, mid_high.shape[2]), 0)
    column_rank = ranks[col]

    def middle(s, _):
        rank = ranks[order[row * slots + s]]
        kept = (sub < rank) & ((lane < column_rank) | (lane >= width))
        mid_high[s], mid_low[s] = cut_two(jnp.where(kept, both[s], 0.0))
        return 0

    lax.fori_loop(0, slots, middle, 0)
    group = n_col // (slots * 2)
    size = group * left.shape[0]

    def rows(b, _):
        here = rows_l[pl.ds(b * group, group)].reshape(size, width)
        s = b // 2
        value = dot3(cut_two(here), (mid_high[s], mid_low[s]), ((1,), (0,)))
        place = pl.ds(pl.multiple_of(b * size, size), size)
        a_high[place], a_low[place] = cut_two(value[:, :width])
        a_rest[place] = value[:, width:]
        return 0

    lax.fori_loop(0, slots * 2, rows, 0)
    left_unit(3, most, l_three)

    def drain(d, _):
        def one(src, side):
            for p in range(late):
                y_copy(p, src, src * ACROSS + y).wait_send()
            for p in range(late + 1):
                along(side, lambda way: z_copy(p, src, way).wait_send())
            along(side, lambda way: z_copy(late, src, way, True).wait_send())

        sources(d, one)
        return 0

    for p in range(late + 1):
        y_copy(p, z, col).wait_send()
        upward(lambda way: z_copy(p, z, way).wait_send())
        downward(lambda way: z_copy(p, z, way).wait_send())
    upward(lambda way: z_copy(late, z, way, True).wait_send())
    downward(lambda way: z_copy(late, z, way, True).wait_send())
    lax.fori_loop(1, length, drain, 0)

    def finish(u, _):
        r_drain(u)
        return 0

    lax.fori_loop(0, n_col, finish, 0)
    for copy in held:
        copy.wait()

    def finish_left(u, _):
        l_drain(u)
        l_ready(u)
        return 0

    lax.fori_loop(0, tile_l.shape[0] * 2, finish_left, 0)


def gather(n_row, n_col, order, ranks, left, right, solved, trailing, sides_in):
    slots, depth, width = right.shape
    length = n_col // ACROSS
    teams = n_row // CORES
    f32 = jnp.float32
    lrows = left.shape[0]
    lefts = n_col // slots
    vmem = pl.BlockSpec(memory_space=pltpu.VMEM)
    hbm = pl.BlockSpec(memory_space=pltpu.HBM)
    smem = pl.BlockSpec(memory_space=pltpu.SMEM)
    dma = pltpu.SemaphoreType.DMA
    r_units, r_part = n_col, (depth // CORES, width)
    l_units, l_part = 2 * lefts, (lrows // 2 // CORES, width)

    def buffers(units, part):
        return [pltpu.VMEM((units,) + part, f32)] * 3 + [pltpu.VMEM((teams, units) + part, f32)]

    def sems(units):
        return [dma((units,)), dma((units,)), dma((teams, units)), dma((teams, units)), dma((units,)), dma((units,))]

    return pl.pallas_call(
        functools.partial(gather_kernel, n_row, n_col, slots),
        out_shape=(
            jax.ShapeDtypeStruct((n_col * lrows, width), jnp.bfloat16),
            jax.ShapeDtypeStruct((n_col * lrows, width), jnp.bfloat16),
            jax.ShapeDtypeStruct((n_col * lrows, solved.shape[1]), f32),
            jax.ShapeDtypeStruct((lefts,) + left.shape, f32),
            jax.ShapeDtypeStruct(trailing.shape, f32),
            jax.ShapeDtypeStruct(sides_in.shape, f32),
        ),
        in_specs=[smem, smem, hbm, hbm, hbm, hbm, hbm],
        out_specs=(vmem,) * 6,
        scratch_shapes=[
            pltpu.VMEM((n_col,) + left.shape, f32),
            pltpu.VMEM((slots, n_col, depth, width), f32),
            pltpu.VMEM((n_col, depth, width), f32),
            pltpu.VMEM((n_row * solved.shape[0], solved.shape[1]), f32),
            pltpu.VMEM((slots, width, width + solved.shape[1]), f32),
            pltpu.VMEM((slots, width, width + solved.shape[1]), jnp.bfloat16),
            pltpu.VMEM((slots, width, width + solved.shape[1]), jnp.bfloat16),
            *buffers(r_units, r_part),
            *buffers(l_units, l_part),
            dma((slots + 2,)),
            dma((2,)),
            dma((slots + 2, n_col)),
            dma((2, slots + 3, length)),
            dma((slots + 2, length)),
            dma((n_row,)),
            dma((n_row,)),
            *sems(r_units),
            *sems(l_units),
        ],
        compiler_params=pltpu.CompilerParams(collective_id=0, has_side_effects=True, vmem_limit_bytes=GATHER_VMEM),
        name="gather_panel",
    )(*(pltpu.with_memory_space_constraint(a, pltpu.HBM) for a in (order, ranks, left, right, solved, trailing, sides_in)))


def cut_two(x):
    high = x.astype(jnp.bfloat16)
    return high, (x - high.astype(jnp.float32)).astype(jnp.bfloat16)


def dot3(a, b, dims):
    (ah, al), (bh, bl) = a, b

    def dot(u, v):
        return lax.dot_general(u, v, (dims, ((), ())), preferred_element_type=jnp.float32)

    return dot(ah, bh) + (dot(ah, bl) + dot(al, bh))


def update_kernel(a_high, a_low, a_rest, tile, trailing, sides_in, trail_out, rhs_out, tile_high, tile_low):
    @pl.when(pl.program_id(0) == 0)
    def _():
        tile_high[...], tile_low[...] = cut_two(tile[...].reshape(tile_high.shape))

    change = dot3((a_high[...], a_low[...]), (tile_high[...], tile_low[...]), ((1,), (1,)))
    trail_out[...] = trailing[...] - change
    rhs_out[...] = sides_in[...] - a_rest[...]


def update(a_high, a_low, a_rest, tile, trailing, right_sides):
    rows, columns = trailing.shape
    width, others = a_high.shape[1], right_sides.shape[1]
    blocks = 4
    size = rows // blocks

    def block(wide):
        return pl.BlockSpec((size, wide), lambda i: (i, 0))

    return pl.pallas_call(
        update_kernel,
        grid=(blocks,),
        out_shape=(jax.ShapeDtypeStruct(trailing.shape, jnp.float32), jax.ShapeDtypeStruct(right_sides.shape, jnp.float32)),
        in_specs=[block(width), block(width), block(others), pl.BlockSpec(tile.shape, lambda i: (0, 0, 0)), block(columns), block(others)],
        out_specs=(block(columns), block(others)),
        scratch_shapes=[pltpu.VMEM((columns, width), jnp.bfloat16)] * 2,
        compiler_params=pltpu.CompilerParams(vmem_limit_bytes=UPDATE_VMEM),
        name="update_panel",
    )(a_high, a_low, a_rest, tile, trailing, right_sides)


def on_device(n_row, n_col, trailing, panel_left, panel_right, panel_solved, right_sides, tile_ranks, tile_order):
    parts = gather(n_row, n_col, tile_order, tile_ranks, panel_left, panel_right, panel_solved, trailing, right_sides)
    return update(*parts)


def solution(mesh):
    return jax.shard_map(
        functools.partial(on_device, mesh.shape["row"], mesh.shape["col"]),
        mesh=mesh,
        in_specs=(
            P("row", "col"),
            P(("row", "col"), None),
            P("row", "col", None),
            P("row", "col"),
            P("row", "col"),
            P(),
            P(),
        ),
        out_specs=(P("row", "col"), P("row", "col")),
        check_vma=False,
    )
```

```python
import functools

import jax
import jax.numpy as jnp
from jax import lax
from jax.experimental import pallas as pl
from jax.experimental.pallas import tpu as pltpu
from jax.sharding import PartitionSpec as P

MESH = pl.DeviceIdType.MESH
ACROSS = 2
CORES = 2
GATHER_VMEM = 30 * 1024 * 1024
UPDATE_VMEM = 16 * 1024 * 1024


def find(order, value):
    place = jnp.int32(0)
    for i in range(order.shape[0]):
        place = jnp.where(order[i] == value, jnp.int32(i), place)
    return place


def chain(where, root_row, root_team, candidate, tile_at, first_out, first_in, chip, far_in, sends, fr, xr, tr):
    row, col, team, core, teams = where
    pair = team * CORES + (1 - core)

    def to_pair(src, dst, sem):
        return pltpu.make_async_remote_copy(src, dst, sends.at[0], sem, device_id=(pair, col), device_id_type=MESH)

    def f_copy(u):
        return to_pair(first_out.at[u], first_in.at[u], fr.at[u])

    def x_copy(u, k):
        to = lax.rem(team + k, teams)
        return pltpu.make_async_remote_copy(chip.at[u], far_in.at[k - 1, u], sends.at[k], xr.at[k - 1, u], device_id=(to * CORES + core, col), device_id_type=MESH)

    def t_copy(u, which):
        ref = tile_at(u, which)
        return pltpu.make_async_remote_copy(ref, ref, sends.at[teams], tr.at[u], device_id=(pair, col), device_id_type=MESH)

    def one(u):
        first_out[u] = candidate(u, 1 - core)
        f_copy(u).start()

    def two(u):
        mine = candidate(u, core)
        f_copy(u).wait_recv()
        chip[u] = jnp.where(root_row == row, mine, first_in[u])
        for k in range(1, teams):
            x_copy(u, k).start()

    def three(u):
        value = chip[u]
        for k in range(1, teams):
            x_copy(u, k).wait_recv()
            value = jnp.where(root_team == lax.rem(team + teams - k, teams), far_in[k - 1, u], value)
        tile_at(u, core)[...] = value
        t_copy(u, core).start()

    def ready(u):
        t_copy(u, 1 - core).wait_recv()

    def drain():
        for k in range(teams + 1):
            pltpu.make_async_remote_copy(chip, chip, sends.at[k], fr.at[0], device_id=(pair, col), device_id_type=MESH).wait_send()

    return one, two, three, ready, drain


def gather_kernel(n_row, n_col, slots, order, ranks, left, right, solved, trailing, sides_in, a_high, a_low, a_rest, tile_l, trail_here, sides_here,
                  rows_l, rows_r, tile_r, rows_w, both, mid_high, mid_low, rf_out, rf_in, r_chip, r_far, lf_out, lf_in, l_chip, l_far,
                  own_sem, held_sem, rsem, zsem, ysem, wsem, wrsem, r_sends, rfr, rxr, rtr, l_sends, lfr, lxr, ltr):
    length = n_col // ACROSS
    half = length // slots
    teams = n_row // CORES
    depth, width = rows_r.shape[2], rows_r.shape[3]
    cut = left.shape[0] // 2
    early, late = slots, slots + 1
    row, col = lax.axis_index("row"), lax.axis_index("col")
    z, y = col // ACROSS, col % ACROSS
    team, core = row // CORES, row % CORES
    mate = z * ACROSS + (1 - y)
    last_up, last_down = z, length - 1 - z
    most = jnp.maximum(last_up, last_down)
    through = ((z > 0) & (z < length - 1)).astype(jnp.int32)

    barrier = pltpu.get_barrier_semaphore()

    def greet(r, c):
        pl.semaphore_signal(barrier, inc=1, device_id=(r, c), device_id_type=MESH)

    @pl.when(z > 0)
    def _():
        greet(row, col - ACROSS)

    @pl.when(z < length - 1)
    def _():
        greet(row, col + ACROSS)

    greet(row, mate)
    for k in range(1, n_row):
        greet(lax.rem(row + k, n_row), col)

    def w_rows(r):
        size = solved.shape[0]
        return rows_w.at[pl.ds(pl.multiple_of(r * size, size), size)]

    own = [
        pltpu.make_async_copy(right, rows_r.at[:, col], own_sem.at[0]),
        pltpu.make_async_copy(left, rows_l.at[col], own_sem.at[1]),
        pltpu.make_async_copy(solved, w_rows(row), own_sem.at[2]),
    ]
    for copy in own:
        copy.start()
    pl.semaphore_wait(barrier, (z > 0).astype(jnp.int32) + (z < length - 1).astype(jnp.int32) + n_row)

    def piece(p, c):
        if p == early:
            return rows_l.at[c, pl.ds(0, cut)]
        if p == late:
            return rows_l.at[c, pl.ds(cut, cut)]
        return rows_r.at[p, c]

    def mine(p):
        if p == early:
            return left.at[pl.ds(0, cut)]
        if p == late:
            return left.at[pl.ds(cut, cut)]
        return right.at[p]

    def z_copy(p, src, way, across=False, fresh=False):
        c = src * ACROSS + ((1 - y) if across else y)
        lane = 0 if p < slots else 1
        to = col + (ACROSS if way == 0 else -ACROSS)
        return pltpu.make_async_remote_copy(mine(p) if fresh else piece(p, c), piece(p, c), zsem.at[lane, way, src], rsem.at[p, c], device_id=(row, to), device_id_type=MESH)

    def y_copy(p, src, c, fresh=False):
        return pltpu.make_async_remote_copy(mine(p) if fresh else piece(p, c), piece(p, c), ysem.at[max(p - slots + 1, 0)], rsem.at[p, c], device_id=(row, mate), device_id_type=MESH)

    def w_copy(k):
        return pltpu.make_async_remote_copy(solved, w_rows(row), wsem.at[0], wrsem.at[0], device_id=(lax.rem(row + k, n_row), col), device_id_type=MESH)

    def upward(act):
        pl.when(z < length - 1)(functools.partial(act, 0))

    def downward(act):
        pl.when(z > 0)(functools.partial(act, 1))

    def along(side, act):
        (upward if side == 0 else downward)(act)

    def sources(d, body):
        for side in range(2):
            src = z - d if side == 0 else z + d
            ok = (src >= 0) if side == 0 else (src < length)
            pl.when(ok & (d > 0))(functools.partial(body, src, side))

    def near(d, body):
        @pl.when(d == 0)
        def _():
            body(col)

        sources(d, lambda src, side: body(src * ACROSS + y))

    def far(d, body):
        @pl.when(d == 0)
        def _():
            body(mate)

        sources(d, lambda src, side: body(src * ACROSS + 1 - y))

    root_slot = find(order, col)
    local = lax.rem(root_slot, slots)
    root_row = root_slot // slots
    root_team = root_row // CORES
    where = (row, col, team, core, teams)

    def pick(parts):
        value = parts[0]
        for s in range(1, slots):
            value = jnp.where(local == s, parts[s], value)
        return value

    part = depth // CORES

    def rows_of(which):
        return pl.ds(pl.multiple_of(which * part, part), part)

    def r_candidate(c, which):
        return pick([rows_r[s, c, rows_of(which)] for s in range(slots)])

    r_one, r_two, r_three, r_ready, r_drain = chain(
        where, root_row, root_team, r_candidate, lambda c, which: tile_r.at[c, rows_of(which)],
        rf_out, rf_in, r_chip, r_far, r_sends, rfr, rxr, rtr)

    lpart = cut // CORES

    def l_rows(u, which):
        return pl.ds(pl.multiple_of((u % 2) * cut + which * lpart, lpart), lpart)

    def l_candidate(u, which):
        return pick([rows_l[u // 2 + s * half * ACROSS, l_rows(u, which)] for s in range(slots)])

    l_one, l_two, l_three, l_ready, l_drain = chain(
        where, root_row, root_team, l_candidate, lambda u, which: tile_l.at[u // 2, l_rows(u, which)],
        lf_out, lf_in, l_chip, l_far, l_sends, lfr, lxr, ltr)

    def lefts(d, across, which, body):
        def one(q, _):
            last = jnp.abs(z - q)
            for s in range(1, slots):
                last = jnp.maximum(last, jnp.abs(z - q - s * half))

            @pl.when(last == d)
            def _():
                body((q * ACROSS + ((1 - y) if across else y)) * 2 + which)

            return 0

        lax.fori_loop(0, half, one, 0)

    def arrived(p, c):
        ref = piece(p, c)
        pltpu.make_async_remote_copy(ref, ref, ysem.at[0], rsem.at[p, c], device_id=(row, mate), device_id_type=MESH).wait_recv()

    for s in range(slots):
        upward(lambda way: z_copy(s, z, way, fresh=True).start())
        downward(lambda way: z_copy(s, z, way, fresh=True).start())
        y_copy(s, z, col, fresh=True).start()
    y_copy(late, z, col, fresh=True).start()
    for k in range(1, n_row):
        w_copy(k).start()

    def send_left(way):
        z_copy(early, z, way, fresh=True).start()
        z_copy(late, z, way, fresh=True).start()

    @pl.when((last_up == 0) & (z < length - 1))
    def _():
        send_left(0)

    @pl.when((last_down == 0) & (z > 0))
    def _():
        send_left(1)

    both[...] = jnp.zeros_like(both)
    for copy in own:
        copy.wait()
    r_one(col)
    r_two(col)

    held = [pltpu.make_async_copy(trailing, trail_here, held_sem.at[0]), pltpu.make_async_copy(sides_in, sides_here, held_sem.at[1])]
    for copy in held:
        copy.start()

    def relay_rights(t):
        for s in range(slots):
            def one(src, side, s=s):
                arrived(s, src * ACROSS + y)
                along(side, lambda way: z_copy(s, src, way).start())
                y_copy(s, src, src * ACROSS + y).start()

            sources(t, one)

    def own_lefts(t):
        @pl.when((t == last_up) & (z < length - 1))
        def _():
            send_left(0)

        @pl.when((t == last_down) & (z > 0))
        def _():
            send_left(1)

        @pl.when(t == 2)
        def _():
            arrived(late, mate)

        @pl.when((t == jnp.maximum(last_up, 2)) & (z < length - 1))
        def _():
            z_copy(late, z, 0, True).start()

        @pl.when((t == jnp.maximum(last_down, 2)) & (z > 0))
        def _():
            z_copy(late, z, 1, True).start()

        @pl.when(t == most)
        def _():
            y_copy(early, z, col, fresh=True).start()

    def left_arrives(k, d):
        def one(src, side):
            if k == 0:
                arrived(early, src * ACROSS + y)
                y_copy(early, src, src * ACROSS + y).start()
                along(side, lambda way: z_copy(early, src, way).start())
            elif k == 1:
                arrived(late, src * ACROSS + y)
                along(side, lambda way: z_copy(late, src, way).start())
            elif k == 2:
                arrived(late, src * ACROSS + 1 - y)
                along(side, lambda way: z_copy(late, src, way, True).start())
            else:
                arrived(early, src * ACROSS + 1 - y)

        sources(d, one)

    def left_unit(k, d, body):
        lefts(d, k >= 2, 1 if k in (1, 2) else 0, body)

    def w_wait():
        ref = rows_w.at[pl.ds(0, (n_row - 1) * solved.shape[0])]
        pltpu.make_async_remote_copy(ref, ref, wsem.at[0], wrsem.at[0], device_id=(row, mate), device_id_type=MESH).wait()

    def accumulate(d):
        def one(src, _):
            @pl.when(jnp.abs(z - src) == d)
            def _():
                for across in range(ACROSS):
                    r_ready(src * ACROSS + across)
                start = pl.multiple_of(src * (ACROSS * depth), ACROSS * depth)
                column = tile_r[pl.ds(src * ACROSS, ACROSS)].reshape(ACROSS * depth, width)
                column = cut_two(jnp.concatenate([column, rows_w[pl.ds(start, ACROSS * depth)]], axis=1))
                for s in range(slots):
                    rows = cut_two(rows_r[s, pl.ds(src * ACROSS, ACROSS)].reshape(ACROSS * depth, width))
                    both[s] += dot3(rows, column, ((0,), (0,)))

            return 0

        lax.fori_loop(0, length, one, 0)

    first_last = jnp.minimum(most, 2)

    def step(t, _):
        a = jnp.where(through == 1, t - most + 1, 0)
        b = jnp.where(through == 1, 0, t - most + 1)
        c = t - most + through
        e = t - most - through
        relay_rights(t)
        own_lefts(t)
        near(t, r_one)
        left_arrives(0, a)
        left_unit(0, a, l_one)
        left_arrives(1, a)
        left_unit(1, a, l_one)
        left_unit(0, a, l_two)
        left_arrives(2, c)
        left_unit(2, c, l_one)
        left_unit(1, a, l_two)
        near(t, r_two)
        left_arrives(0, b)
        left_unit(0, b, l_one)
        left_arrives(1, b)
        left_unit(1, b, l_one)
        left_unit(0, b, l_two)
        left_unit(2, c, l_two)

        @pl.when(t == 1)
        def _():
            for s in range(slots):
                arrived(s, mate)

        def one(src, side):
            for s in range(slots):
                arrived(s, src * ACROSS + 1 - y)

        sources(t - 1, one)
        far(t - 1, r_one)
        left_unit(1, b, l_two)

        @pl.when(e == first_last)
        def _():
            arrived(early, mate)
            left_arrives(3, 1)
            left_unit(3, 1, l_one)

        @pl.when(e > 1)
        def _():
            left_arrives(3, e)
            left_unit(3, e, l_one)

        far(t - 1, r_two)

        @pl.when(e == first_last)
        def _():
            left_unit(3, 1, l_two)

        @pl.when(e > 1)
        def _():
            left_unit(3, e, l_two)

        @pl.when(t == 2)
        def _():
            w_wait()

        near(t - 1, r_three)
        far(t - 2, r_three)
        accumulate(t - 3)
        return 0

    lax.fori_loop(1, jnp.maximum(2 * most + 1 + through, most + 4), step, 0)

    def spread(d, _):
        for k in range(4):
            left_unit(k, d, l_three)
        return 0

    lax.fori_loop(1, most, spread, 0)
    left_unit(0, most, l_three)
    left_unit(1, most, l_three)

    lane = lax.broadcasted_iota(jnp.int32, (width, mid_high.shape[2]), 1)
    sub = lax.broadcasted_iota(jnp.int32, (width, mid_high.shape[2]), 0)
    column_rank = ranks[col]

    def middle(s, _):
        rank = ranks[order[row * slots + s]]
        kept = (sub < rank) & ((lane < column_rank) | (lane >= width))
        mid_high[s], mid_low[s] = cut_two(jnp.where(kept, both[s], 0.0))
        return 0

    lax.fori_loop(0, slots, middle, 0)
    group = n_col // (slots * 2)
    size = group * left.shape[0]

    def rows(b, _):
        here = rows_l[pl.ds(b * group, group)].reshape(size, width)
        s = b // 2
        value = dot3(cut_two(here), (mid_high[s], mid_low[s]), ((1,), (0,)))
        place = pl.ds(pl.multiple_of(b * size, size), size)
        a_high[place], a_low[place] = cut_two(value[:, :width])
        a_rest[place] = value[:, width:]
        return 0

    lax.fori_loop(0, slots * 2, rows, 0)
    left_unit(2, most, l_three)
    left_unit(3, most, l_three)

    def leave(ref, sem):
        pltpu.make_async_remote_copy(ref, ref, sem, rsem.at[0, 0], device_id=(row, mate), device_id_type=MESH).wait_send()

    def drain(src, _):
        @pl.when((src <= z) & (z < length - 1))
        def _():
            leave(rows_r.at[:, 0], zsem.at[0, 0, src])
            leave(rows_l.at[pl.ds(0, 3), pl.ds(0, cut)], zsem.at[1, 0, src])

        @pl.when((src >= z) & (z > 0))
        def _():
            leave(rows_r.at[:, 0], zsem.at[0, 1, src])
            leave(rows_l.at[pl.ds(0, 3), pl.ds(0, cut)], zsem.at[1, 1, src])

        return 0

    lax.fori_loop(0, length, drain, 0)
    leave(rows_r.at[:, pl.ds(0, length)], ysem.at[0])
    leave(rows_l.at[pl.ds(0, length), pl.ds(0, cut)], ysem.at[1])
    leave(rows_l.at[0, pl.ds(0, cut)], ysem.at[2])
    r_drain()
    l_drain()

    def finish_left(u, _):
        l_ready(u)
        return 0

    lax.fori_loop(0, tile_l.shape[0] * 2, finish_left, 0)
    for copy in held:
        copy.wait()


def gather(n_row, n_col, order, ranks, left, right, solved, trailing, sides_in):
    slots, depth, width = right.shape
    length = n_col // ACROSS
    teams = n_row // CORES
    f32 = jnp.float32
    lrows = left.shape[0]
    lefts = n_col // slots
    vmem = pl.BlockSpec(memory_space=pltpu.VMEM)
    hbm = pl.BlockSpec(memory_space=pltpu.HBM)
    smem = pl.BlockSpec(memory_space=pltpu.SMEM)
    dma = pltpu.SemaphoreType.DMA
    r_units, r_part = n_col, (depth // CORES, width)
    l_units, l_part = 2 * lefts, (lrows // 2 // CORES, width)

    def buffers(units, part):
        return [pltpu.VMEM((units,) + part, f32)] * 3 + [pltpu.VMEM((teams - 1, units) + part, f32)]

    def sems(units):
        return [dma((teams + 1,)), dma((units,)), dma((teams - 1, units)), dma((units,))]

    return pl.pallas_call(
        functools.partial(gather_kernel, n_row, n_col, slots),
        out_shape=(
            jax.ShapeDtypeStruct((n_col * lrows, width), jnp.bfloat16),
            jax.ShapeDtypeStruct((n_col * lrows, width), jnp.bfloat16),
            jax.ShapeDtypeStruct((n_col * lrows, solved.shape[1]), f32),
            jax.ShapeDtypeStruct((lefts,) + left.shape, f32),
            jax.ShapeDtypeStruct(trailing.shape, f32),
            jax.ShapeDtypeStruct(sides_in.shape, f32),
        ),
        in_specs=[smem, smem, hbm, hbm, hbm, hbm, hbm],
        out_specs=(vmem,) * 6,
        scratch_shapes=[
            pltpu.VMEM((n_col,) + left.shape, f32),
            pltpu.VMEM((slots, n_col, depth, width), f32),
            pltpu.VMEM((n_col, depth, width), f32),
            pltpu.VMEM((n_row * solved.shape[0], solved.shape[1]), f32),
            pltpu.VMEM((slots, width, width + solved.shape[1]), f32),
            pltpu.VMEM((slots, width, width + solved.shape[1]), jnp.bfloat16),
            pltpu.VMEM((slots, width, width + solved.shape[1]), jnp.bfloat16),
            *buffers(r_units, r_part),
            *buffers(l_units, l_part),
            dma((3,)),
            dma((2,)),
            dma((slots + 2, n_col)),
            dma((2, 2, length)),
            dma((3,)),
            dma((1,)),
            dma((1,)),
            *sems(r_units),
            *sems(l_units),
        ],
        compiler_params=pltpu.CompilerParams(collective_id=0, has_side_effects=True, vmem_limit_bytes=GATHER_VMEM),
        name="gather_panel",
    )(*(pltpu.with_memory_space_constraint(a, pltpu.HBM) for a in (order, ranks, left, right, solved, trailing, sides_in)))


def cut_two(x):
    high = x.astype(jnp.bfloat16)
    return high, (x - high.astype(jnp.float32)).astype(jnp.bfloat16)


def dot3(a, b, dims):
    (ah, al), (bh, bl) = a, b

    def dot(u, v):
        return lax.dot_general(u, v, (dims, ((), ())), preferred_element_type=jnp.float32)

    return dot(ah, bh) + (dot(ah, bl) + dot(al, bh))


def update_kernel(a_high, a_low, a_rest, tile, trailing, sides_in, trail_out, rhs_out, tile_high, tile_low):
    @pl.when(pl.program_id(0) == 0)
    def _():
        tile_high[...], tile_low[...] = cut_two(tile[...].reshape(tile_high.shape))

    change = dot3((a_high[...], a_low[...]), (tile_high[...], tile_low[...]), ((1,), (1,)))
    trail_out[...] = trailing[...] - change
    rhs_out[...] = sides_in[...] - a_rest[...]


def update(a_high, a_low, a_rest, tile, trailing, right_sides):
    rows, columns = trailing.shape
    width, others = a_high.shape[1], right_sides.shape[1]
    blocks = 4
    size = rows // blocks

    def block(wide):
        return pl.BlockSpec((size, wide), lambda i: (i, 0))

    return pl.pallas_call(
        update_kernel,
        grid=(blocks,),
        out_shape=(jax.ShapeDtypeStruct(trailing.shape, jnp.float32), jax.ShapeDtypeStruct(right_sides.shape, jnp.float32)),
        in_specs=[block(width), block(width), block(others), pl.BlockSpec(tile.shape, lambda i: (0, 0, 0)), block(columns), block(others)],
        out_specs=(block(columns), block(others)),
        scratch_shapes=[pltpu.VMEM((columns, width), jnp.bfloat16)] * 2,
        compiler_params=pltpu.CompilerParams(vmem_limit_bytes=UPDATE_VMEM),
        name="update_panel",
    )(a_high, a_low, a_rest, tile, trailing, right_sides)


def on_device(n_row, n_col, trailing, panel_left, panel_right, panel_solved, right_sides, tile_ranks, tile_order):
    parts = gather(n_row, n_col, tile_order, tile_ranks, panel_left, panel_right, panel_solved, trailing, right_sides)
    return update(*parts)


def solution(mesh):
    return jax.shard_map(
        functools.partial(on_device, mesh.shape["row"], mesh.shape["col"]),
        mesh=mesh,
        in_specs=(
            P("row", "col"),
            P(("row", "col"), None),
            P("row", "col", None),
            P("row", "col"),
            P("row", "col"),
            P(),
            P(),
        ),
        out_specs=(P("row", "col"), P("row", "col")),
        check_vma=False,
    )
```

```python
import functools

import jax
import jax.numpy as jnp
from jax import lax
from jax.experimental import pallas as pl
from jax.experimental.pallas import tpu as pltpu
from jax.sharding import PartitionSpec as P

MESH = pl.DeviceIdType.MESH
ACROSS = 2
CORES = 2
GATHER_VMEM = 30 * 1024 * 1024
UPDATE_VMEM = 16 * 1024 * 1024


def find(order, value):
    place = jnp.int32(0)
    for i in range(order.shape[0]):
        place = jnp.where(order[i] == value, jnp.int32(i), place)
    return place


def chain(where, root_row, root_team, candidate, tile_at, group, first_out, first_in, chip, far_in, sends, fr, xr, tr):
    row, col, team, core, teams = where
    pair = team * CORES + (1 - core)

    def to_pair(src, dst, sem):
        return pltpu.make_async_remote_copy(src, dst, sends.at[0], sem, device_id=(pair, col), device_id_type=MESH)

    def f_copy(u):
        return to_pair(first_out.at[u], first_in.at[u], fr.at[u])

    def x_copy(u, k):
        to = lax.rem(team + k, teams)
        return pltpu.make_async_remote_copy(chip.at[u], far_in.at[k - 1, u], sends.at[k], xr.at[k - 1, u], device_id=(to * CORES + core, col), device_id_type=MESH)

    def t_copy(u, which):
        ref = tile_at(u, which)
        return pltpu.make_async_remote_copy(ref, ref, sends.at[teams], tr.at[u // group], device_id=(pair, col), device_id_type=MESH)

    def one(u):
        first_out[u] = candidate(u, 1 - core)
        f_copy(u).start()

    def two(u):
        mine = candidate(u, core)
        f_copy(u).wait_recv()
        chip[u] = jnp.where(root_row == row, mine, first_in[u])
        for k in range(1, teams):
            x_copy(u, k).start()

    def three(u):
        value = chip[u]
        for k in range(1, teams):
            x_copy(u, k).wait_recv()
            value = jnp.where(root_team == lax.rem(team + teams - k, teams), far_in[k - 1, u], value)
        tile_at(u, core)[...] = value
        t_copy(u, core).start()

    def ready(g):
        ref = chip.at[pl.ds(g * group, group)]
        to_pair(ref, ref, tr.at[g]).wait_recv()

    def drain():
        for k in range(teams + 1):
            pltpu.make_async_remote_copy(chip, chip, sends.at[k], fr.at[0], device_id=(pair, col), device_id_type=MESH).wait_send()

    return one, two, three, ready, drain


def gather_kernel(n_row, n_col, slots, order, ranks, left, right, solved, trailing, sides_in, product, tile_l, trail_here, sides_here,
                  rows_l, rows_r, tile_r, rows_w, both, mid, tile_cut, order_here, ranks_here, rf_out, rf_in, r_chip, r_far, lf_out, lf_in, l_chip, l_far,
                  own_sem, held_sem, rsem, zsem, ysem, wsem, wrsem, r_sends, rfr, rxr, rtr, l_sends, lfr, lxr, ltr):
    length = n_col // ACROSS
    half = length // slots
    teams = n_row // CORES
    depth, width = rows_r.shape[2], rows_r.shape[3]
    cut = left.shape[0] // 2
    early, late = slots, slots + 1
    row, col = lax.axis_index("row"), lax.axis_index("col")
    z, y = col // ACROSS, col % ACROSS
    team, core = row // CORES, row % CORES
    mate = z * ACROSS + (1 - y)
    last_up, last_down = z, length - 1 - z
    most = jnp.maximum(last_up, last_down)
    through = ((z > 0) & (z < length - 1)).astype(jnp.int32)

    barrier = pltpu.get_barrier_semaphore()

    def greet(r, c):
        pl.semaphore_signal(barrier, inc=1, device_id=(r, c), device_id_type=MESH)

    @pl.when(z > 0)
    def _():
        greet(row, col - ACROSS)

    @pl.when(z < length - 1)
    def _():
        greet(row, col + ACROSS)

    greet(row, mate)
    for k in range(1, n_row):
        greet(lax.rem(row + k, n_row), col)

    def w_rows(r):
        size = solved.shape[0]
        return rows_w.at[pl.ds(pl.multiple_of(r * size, size), size)]

    own = [
        pltpu.make_async_copy(right, rows_r.at[:, col], own_sem.at[0]),
        pltpu.make_async_copy(left, rows_l.at[col], own_sem.at[1]),
        pltpu.make_async_copy(solved, w_rows(row), own_sem.at[2]),
        pltpu.make_async_copy(order, order_here, own_sem.at[3]),
        pltpu.make_async_copy(ranks, ranks_here, own_sem.at[4]),
    ]
    for copy in own:
        copy.start()
    pl.semaphore_wait(barrier, (z > 0).astype(jnp.int32) + (z < length - 1).astype(jnp.int32) + n_row)

    def piece(p, c):
        if p == early:
            return rows_l.at[c, pl.ds(0, cut)]
        if p == late:
            return rows_l.at[c, pl.ds(cut, cut)]
        return rows_r.at[p, c]

    def mine(p):
        if p == early:
            return left.at[pl.ds(0, cut)]
        if p == late:
            return left.at[pl.ds(cut, cut)]
        return right.at[p]

    def z_copy(p, src, way, across=False, fresh=False):
        c = src * ACROSS + ((1 - y) if across else y)
        lane = 0 if p < slots else (2 if across else 1)
        to = col + (ACROSS if way == 0 else -ACROSS)
        return pltpu.make_async_remote_copy(mine(p) if fresh else piece(p, c), piece(p, c), zsem.at[way, lane], rsem.at[p, c], device_id=(row, to), device_id_type=MESH)

    def y_copy(p, src, c, fresh=False):
        return pltpu.make_async_remote_copy(mine(p) if fresh else piece(p, c), piece(p, c), ysem.at[max(p - slots + 1, 0)], rsem.at[p, c], device_id=(row, mate), device_id_type=MESH)

    def w_copy(k):
        return pltpu.make_async_remote_copy(solved, w_rows(row), wsem.at[0], wrsem.at[0], device_id=(lax.rem(row + k, n_row), col), device_id_type=MESH)

    def upward(act):
        pl.when(z < length - 1)(functools.partial(act, 0))

    def downward(act):
        pl.when(z > 0)(functools.partial(act, 1))

    def along(side, act):
        (upward if side == 0 else downward)(act)

    def sources(d, body):
        for side in range(2):
            src = z - d if side == 0 else z + d
            ok = (src >= 0) if side == 0 else (src < length)
            pl.when(ok & (d > 0))(functools.partial(body, src, side))

    def near(d, body):
        @pl.when(d == 0)
        def _():
            body(col)

        sources(d, lambda src, side: body(src * ACROSS + y))

    def far(d, body):
        @pl.when(d == 0)
        def _():
            body(mate)

        sources(d, lambda src, side: body(src * ACROSS + 1 - y))

    where = (row, col, team, core, teams)

    def lefts(d, across, which, body):
        def one(q, _):
            last = jnp.abs(z - q)
            for s in range(1, slots):
                last = jnp.maximum(last, jnp.abs(z - q - s * half))

            @pl.when(last == d)
            def _():
                body((q * ACROSS + ((1 - y) if across else y)) * 2 + which)

            return 0

        lax.fori_loop(0, half, one, 0)

    def arrived(p, c):
        ref = piece(p, c)
        pltpu.make_async_remote_copy(ref, ref, ysem.at[0], rsem.at[p, c], device_id=(row, mate), device_id_type=MESH).wait_recv()

    for s in range(slots):
        upward(lambda way: z_copy(s, z, way, fresh=True).start())
        downward(lambda way: z_copy(s, z, way, fresh=True).start())
        y_copy(s, z, col, fresh=True).start()
    y_copy(late, z, col, fresh=True).start()
    for k in range(1, n_row):
        w_copy(k).start()

    def send_left(way):
        z_copy(early, z, way, fresh=True).start()
        z_copy(late, z, way, fresh=True).start()

    @pl.when((last_up == 0) & (z < length - 1))
    def _():
        send_left(0)

    @pl.when((last_down == 0) & (z > 0))
    def _():
        send_left(1)

    both[...] = jnp.zeros_like(both)
    for copy in own:
        copy.wait()

    root_slot = find(order_here, col)
    local = lax.rem(root_slot, slots)
    root_row = root_slot // slots
    root_team = root_row // CORES
    def pick(parts):
        value = parts[0]
        for s in range(1, slots):
            value = jnp.where(local == s, parts[s], value)
        return value

    part = depth // CORES

    def rows_of(which):
        return pl.ds(pl.multiple_of(which * part, part), part)

    def r_candidate(c, which):
        return pick([rows_r[s, c, rows_of(which)] for s in range(slots)])

    r_one, r_two, r_three, r_ready, r_drain = chain(
        where, root_row, root_team, r_candidate, lambda c, which: tile_r.at[c, rows_of(which)], ACROSS,
        rf_out, rf_in, r_chip, r_far, r_sends, rfr, rxr, rtr)

    lpart = cut // CORES

    def l_rows(u, which):
        return pl.ds(pl.multiple_of((u % 2) * cut + which * lpart, lpart), lpart)

    def l_candidate(u, which):
        return pick([rows_l[u // 2 + s * half * ACROSS, l_rows(u, which)] for s in range(slots)])

    l_one, l_two, l_three, l_ready, l_drain = chain(
        where, root_row, root_team, l_candidate, lambda u, which: tile_l.at[u // 2, l_rows(u, which)], tile_l.shape[0],
        lf_out, lf_in, l_chip, l_far, l_sends, lfr, lxr, ltr)

    r_one(col)
    r_two(col)

    held = [pltpu.make_async_copy(trailing, trail_here, held_sem.at[0]), pltpu.make_async_copy(sides_in, sides_here, held_sem.at[1])]
    for copy in held:
        copy.start()

    def relay_rights(t):
        for s in range(slots):
            def one(src, side, s=s):
                arrived(s, src * ACROSS + y)
                along(side, lambda way: z_copy(s, src, way).start())
                y_copy(s, src, src * ACROSS + y).start()

            sources(t, one)

    def own_lefts(t):
        @pl.when((t == last_up) & (z < length - 1))
        def _():
            send_left(0)

        @pl.when((t == last_down) & (z > 0))
        def _():
            send_left(1)

        @pl.when(t == 2)
        def _():
            arrived(late, mate)

        @pl.when((t == jnp.maximum(last_up, 2)) & (z < length - 1))
        def _():
            z_copy(late, z, 0, True).start()

        @pl.when((t == jnp.maximum(last_down, 2)) & (z > 0))
        def _():
            z_copy(late, z, 1, True).start()

        @pl.when(t == most)
        def _():
            y_copy(early, z, col, fresh=True).start()

    def left_arrives(k, d):
        def one(src, side):
            if k == 0:
                arrived(early, src * ACROSS + y)
                y_copy(early, src, src * ACROSS + y).start()
                along(side, lambda way: z_copy(early, src, way).start())
            elif k == 1:
                arrived(late, src * ACROSS + y)
                along(side, lambda way: z_copy(late, src, way).start())
            elif k == 2:
                arrived(late, src * ACROSS + 1 - y)
                along(side, lambda way: z_copy(late, src, way, True).start())
            else:
                arrived(early, src * ACROSS + 1 - y)

        sources(d, one)

    def left_unit(k, d, body):
        lefts(d, k >= 2, 1 if k in (1, 2) else 0, body)

    def w_wait():
        ref = rows_w.at[pl.ds(0, (n_row - 1) * solved.shape[0])]
        pltpu.make_async_remote_copy(ref, ref, wsem.at[0], wrsem.at[0], device_id=(row, mate), device_id_type=MESH).wait()

    def accumulate(d):
        def one(src, _):
            @pl.when(jnp.abs(z - src) == d)
            def _():
                r_ready(src)
                start = pl.multiple_of(src * (ACROSS * depth), ACROSS * depth)
                column = tile_r[pl.ds(src * ACROSS, ACROSS)].reshape(ACROSS * depth, width)
                column = cut_right(jnp.concatenate([column, rows_w[pl.ds(start, ACROSS * depth)]], axis=1), 0)
                rows = [rows_r[s, pl.ds(src * ACROSS, ACROSS)].reshape(ACROSS * depth, width) for s in range(slots)]
                both[...] += dot(cut_left(jnp.concatenate(rows, axis=1), 0), column, ((0,), (0,)))

            return 0

        lax.fori_loop(0, length, one, 0)

    first = jnp.minimum(most, 2)

    def other_early(d):
        @pl.when(d == first)
        def _():
            arrived(early, mate)
            left_arrives(3, 1)
            left_unit(3, 1, l_one)

        @pl.when(d > 1)
        def _():
            left_arrives(3, d)
            left_unit(3, d, l_one)

    def other_early_two(d):
        @pl.when(d == first)
        def _():
            left_unit(3, 1, l_two)

        @pl.when(d > 1)
        def _():
            left_unit(3, d, l_two)

    def step(t, _):
        a = jnp.where(through == 1, t - most + 1, 0)
        b = jnp.where(through == 1, 0, t - most + 1)
        c = jnp.where(through == 1, t - most + 1, jnp.where(t < 2 * most, t - most, 0))
        e = jnp.where(t - through < 2 * most, t - most - through, 0)
        relay_rights(t)
        own_lefts(t)
        near(t, r_one)
        left_arrives(0, a)
        left_unit(0, a, l_one)
        left_arrives(1, a)
        left_unit(1, a, l_one)
        left_unit(0, a, l_two)
        left_arrives(2, c)
        left_unit(2, c, l_one)
        left_unit(1, a, l_two)
        near(t, r_two)
        left_arrives(0, b)
        left_unit(0, b, l_one)
        left_unit(2, c, l_two)
        left_unit(0, b, l_two)
        left_arrives(1, b)
        left_unit(1, b, l_one)

        @pl.when(t == 1)
        def _():
            for s in range(slots):
                arrived(s, mate)

        def one(src, side):
            for s in range(slots):
                arrived(s, src * ACROSS + 1 - y)

        sources(t - 1, one)
        far(t - 1, r_one)
        left_unit(1, b, l_two)
        near(t - 1, r_three)
        far(t - 2, r_three)
        far(t - 1, r_two)
        other_early(e)

        @pl.when(t == 2)
        def _():
            w_wait()

        accumulate(jnp.where(t - 2 < most, t - 2, -1))
        other_early_two(e)
        return 0

    lax.fori_loop(1, jnp.maximum(2 * most + through, most + 3), step, 0)
    for copy in held:
        copy.wait()

    lane = lax.broadcasted_iota(jnp.int32, (width, mid.shape[2]), 1)
    sub = lax.broadcasted_iota(jnp.int32, (width, mid.shape[2]), 0)
    column_rank = ranks_here[col]

    def middle(s, _):
        rank = ranks_here[order_here[row * slots + s]]
        kept = (sub < rank) & ((lane < column_rank) | (lane >= width))
        mid[s] = cut_right(jnp.where(kept, both[pl.ds(pl.multiple_of(s * width, width), width)], 0.0), 0)
        return 0

    group = n_col // slots
    size = group * left.shape[0]
    own_slot = z // half

    def rows(i, _):
        b = lax.rem(own_slot + i, slots)
        here = rows_l[pl.ds(b * group, group)].reshape(size, width)
        value = dot(cut_left(here, 1), mid[b], ((1,), (0,)))
        place = pl.ds(pl.multiple_of(b * size, size), size)
        product[place] = cut_left(value[:, :width], 1)
        sides_here[place] -= value[:, width:]
        return 0

    blocks = tile_l.shape[0] // 2
    soon = (2 * z // length) * blocks
    later = blocks - soon

    def spread(u, _):
        l_three(u)
        return 0

    final = jnp.where(through == 1, 0, most)
    left_arrives(2, final)
    left_unit(2, final, l_one)
    other_early(most)
    accumulate(most)
    left_unit(2, final, l_two)
    other_early_two(most)
    lax.fori_loop(0, slots, middle, 0)
    lax.fori_loop(0, 1, rows, 0)
    lax.fori_loop(soon * 2, (soon + blocks) * 2, spread, 0)
    lax.fori_loop(1, slots, rows, 0)
    l_ready(soon // blocks)
    wide = tile_cut.shape[0]
    tile_cut[...] = cut_right(tile_l[pl.ds(soon, blocks)].reshape(wide, width), 1)
    columns = pl.ds(pl.multiple_of(soon * left.shape[0], wide), wide)
    trail_here[:, columns] -= dot(product[...], tile_cut[...], ((1,), (1,)))
    lax.fori_loop(later * 2, (later + blocks) * 2, spread, 0)

    def leave(ref, sem):
        pltpu.make_async_remote_copy(ref, ref, sem, rsem.at[0, 0], device_id=(row, mate), device_id_type=MESH).wait_send()

    for count in range(1, length):
        for way, last in ((0, last_up), (1, last_down)):
            @pl.when(last == count - 1)
            def _(way=way, sent=count):
                leave(rows_r.at[:, pl.ds(0, sent)], zsem.at[way, 0])
                leave(rows_l.at[pl.ds(0, sent)], zsem.at[way, 1])
                leave(rows_l.at[pl.ds(0, sent), pl.ds(0, cut)], zsem.at[way, 2])

    leave(rows_r.at[:, pl.ds(0, length)], ysem.at[0])
    leave(rows_l.at[pl.ds(0, length), pl.ds(0, cut)], ysem.at[1])
    leave(rows_l.at[0, pl.ds(0, cut)], ysem.at[2])
    r_drain()
    l_drain()
    l_ready(later // blocks)


def gather(n_row, n_col, order, ranks, left, right, solved, trailing, sides_in):
    slots, depth, width = right.shape
    length = n_col // ACROSS
    teams = n_row // CORES
    f32 = jnp.float32
    lrows = left.shape[0]
    lefts = n_col // slots
    vmem = pl.BlockSpec(memory_space=pltpu.VMEM)
    hbm = pl.BlockSpec(memory_space=pltpu.HBM)
    dma = pltpu.SemaphoreType.DMA
    r_units, r_part = n_col, (depth // CORES, width)
    l_units, l_part = 2 * lefts, (lrows // 2 // CORES, width)

    def buffers(units, part):
        return [pltpu.VMEM((units,) + part, f32)] * 3 + [pltpu.VMEM((teams - 1, units) + part, f32)]

    def sems(units, group):
        return [dma((teams + 1,)), dma((units,)), dma((teams - 1, units)), dma((units // group,))]

    return pl.pallas_call(
        functools.partial(gather_kernel, n_row, n_col, slots),
        out_shape=(
            jax.ShapeDtypeStruct((n_col * lrows, 3 * width), jnp.bfloat16),
            jax.ShapeDtypeStruct((lefts,) + left.shape, f32),
            jax.ShapeDtypeStruct(trailing.shape, f32),
            jax.ShapeDtypeStruct(sides_in.shape, f32),
        ),
        in_specs=[hbm] * 7,
        out_specs=(vmem,) * 4,
        scratch_shapes=[
            pltpu.VMEM((n_col,) + left.shape, f32),
            pltpu.VMEM((slots, n_col, depth, width), f32),
            pltpu.VMEM((n_col, depth, width), f32),
            pltpu.VMEM((n_row * solved.shape[0], solved.shape[1]), f32),
            pltpu.VMEM((slots * width, width + solved.shape[1]), f32),
            pltpu.VMEM((slots, 3 * width, width + solved.shape[1]), jnp.bfloat16),
            pltpu.VMEM((lefts * lrows // 2, 3 * width), jnp.bfloat16),
            pltpu.SMEM(order.shape, order.dtype),
            pltpu.SMEM(ranks.shape, ranks.dtype),
            *buffers(r_units, r_part),
            *buffers(l_units, l_part),
            dma((5,)),
            dma((2,)),
            dma((slots + 2, n_col)),
            dma((2, 3)),
            dma((3,)),
            dma((1,)),
            dma((1,)),
            *sems(r_units, ACROSS),
            *sems(l_units, lefts),
        ],
        compiler_params=pltpu.CompilerParams(collective_id=0, has_side_effects=True, vmem_limit_bytes=GATHER_VMEM),
        name="gather_panel",
    )(*(pltpu.with_memory_space_constraint(a, pltpu.HBM) for a in (order, ranks, left, right, solved, trailing, sides_in)))


def cut_two(x):
    high = x.astype(jnp.bfloat16)
    return high, (x - high.astype(jnp.float32)).astype(jnp.bfloat16)


def cut_left(x, axis):
    high, low = cut_two(x)
    return jnp.concatenate([high, high, low], axis=axis)


def cut_right(x, axis):
    high, low = cut_two(x)
    return jnp.concatenate([high, low, high], axis=axis)


def dot(a, b, dims):
    return lax.dot_general(a, b, (dims, ((), ())), preferred_element_type=jnp.float32)


def update_kernel(length, product, tile, trailing, sides, trail_out, rhs_out, result, sems):
    rows, wide = result.shape
    blocks = 4
    size = rows // blocks
    soon = (2 * (lax.axis_index("col") // ACROSS)) // length
    here = pl.ds(pl.multiple_of(soon * wide, wide), wide)
    rest = pl.ds(pl.multiple_of((1 - soon) * wide, wide), wide)
    count = tile.shape[0] // 2
    copies = [
        pltpu.make_async_copy(trailing.at[:, here], trail_out.at[:, here], sems.at[0]),
        pltpu.make_async_copy(sides, rhs_out, sems.at[1]),
    ]
    for copy in copies:
        copy.start()
    columns = cut_right(tile[pl.ds((1 - soon) * count, count)].reshape(wide, tile.shape[2]), 1)
    for i in range(blocks):
        place = pl.ds(i * size, size)
        result[place] = trailing[place, rest] - dot(product[place], columns, ((1,), (1,)))
        copies.append(pltpu.make_async_copy(result.at[place], trail_out.at[place, rest], sems.at[2 + i]))
        copies[-1].start()
    for copy in copies:
        copy.wait()


def update(n_col, product, tile, trailing, sides):
    rows, columns = trailing.shape
    vmem = pl.BlockSpec(memory_space=pltpu.VMEM)
    hbm = pl.BlockSpec(memory_space=pltpu.HBM)
    return pl.pallas_call(
        functools.partial(update_kernel, n_col // ACROSS),
        out_shape=(jax.ShapeDtypeStruct(trailing.shape, jnp.float32), jax.ShapeDtypeStruct(sides.shape, jnp.float32)),
        in_specs=[vmem] * 4,
        out_specs=(hbm, hbm),
        scratch_shapes=[pltpu.VMEM((rows, columns // 2), jnp.float32), pltpu.SemaphoreType.DMA((6,))],
        compiler_params=pltpu.CompilerParams(vmem_limit_bytes=UPDATE_VMEM),
        name="update_panel",
    )(product, tile, trailing, sides)


def on_device(n_row, n_col, trailing, panel_left, panel_right, panel_solved, right_sides, tile_ranks, tile_order):
    parts = gather(n_row, n_col, tile_order, tile_ranks, panel_left, panel_right, panel_solved, trailing, right_sides)
    return update(n_col, *parts)


def solution(mesh):
    return jax.shard_map(
        functools.partial(on_device, mesh.shape["row"], mesh.shape["col"]),
        mesh=mesh,
        in_specs=(
            P("row", "col"),
            P(("row", "col"), None),
            P("row", "col", None),
            P("row", "col"),
            P("row", "col"),
            P(),
            P(),
        ),
        out_specs=(P("row", "col"), P("row", "col")),
        check_vma=False,
    )
```

```python
import functools

import jax
import jax.numpy as jnp
from jax import lax
from jax.experimental import pallas as pl
from jax.experimental.pallas import tpu as pltpu
from jax.sharding import PartitionSpec as P

MESH = pl.DeviceIdType.MESH
ACROSS = 2
CORES = 2
GATHER_VMEM = 30 * 1024 * 1024
UPDATE_VMEM = 16 * 1024 * 1024


def find(order, value):
    place = jnp.int32(0)
    for i in range(order.shape[0]):
        place = jnp.where(order[i] == value, jnp.int32(i), place)
    return place


def chain(where, root_row, root_team, candidate, tile_at, group, first_out, first_in, chip, far_in, sends, fr, xr, tr):
    row, col, team, core, teams = where
    pair = team * CORES + (1 - core)

    def to_pair(src, dst, sem):
        return pltpu.make_async_remote_copy(src, dst, sends.at[0], sem, device_id=(pair, col), device_id_type=MESH)

    def f_copy(u):
        return to_pair(first_out.at[u], first_in.at[u], fr.at[u])

    def x_copy(u, k):
        to = lax.rem(team + k, teams)
        return pltpu.make_async_remote_copy(chip.at[u], far_in.at[k - 1, u], sends.at[k], xr.at[k - 1, u], device_id=(to * CORES + core, col), device_id_type=MESH)

    def t_copy(u, which):
        ref = tile_at(u, which)
        return pltpu.make_async_remote_copy(ref, ref, sends.at[teams], tr.at[u // group], device_id=(pair, col), device_id_type=MESH)

    def one(u):
        first_out[u] = candidate(u, 1 - core)
        f_copy(u).start()

    def two(u):
        mine = candidate(u, core)
        f_copy(u).wait_recv()
        chip[u] = jnp.where(root_row == row, mine, first_in[u])
        for k in range(1, teams):
            x_copy(u, k).start()

    def three(u):
        value = chip[u]
        for k in range(1, teams):
            x_copy(u, k).wait_recv()
            value = jnp.where(root_team == lax.rem(team + teams - k, teams), far_in[k - 1, u], value)
        tile_at(u, core)[...] = value
        t_copy(u, core).start()

    def ready(g):
        ref = chip.at[pl.ds(g * group, group)]
        to_pair(ref, ref, tr.at[g]).wait_recv()

    def drain():
        for k in range(teams + 1):
            pltpu.make_async_remote_copy(chip, chip, sends.at[k], fr.at[0], device_id=(pair, col), device_id_type=MESH).wait_send()

    return one, two, three, ready, drain


def gather_kernel(n_row, n_col, slots, order, ranks, left, right, solved, trailing, sides_in, product, tile_l, trail_here, sides_here,
                  rows_l, rows_r, tile_r, rows_w, both, mid, tile_cut, order_here, ranks_here, rf_out, rf_in, r_chip, r_far, lf_out, lf_in, l_chip, l_far,
                  own_sem, held_sem, rsem, zsem, ysem, wsem, wrsem, r_sends, rfr, rxr, rtr, l_sends, lfr, lxr, ltr):
    length = n_col // ACROSS
    half = length // slots
    teams = n_row // CORES
    depth, width = rows_r.shape[2], rows_r.shape[3]
    cut = left.shape[0] // 2
    early, late = slots, slots + 1
    row, col = lax.axis_index("row"), lax.axis_index("col")
    z, y = col // ACROSS, col % ACROSS
    team, core = row // CORES, row % CORES
    mate = z * ACROSS + (1 - y)
    last_up, last_down = z, length - 1 - z
    most = jnp.maximum(last_up, last_down)
    through = ((z > 0) & (z < length - 1)).astype(jnp.int32)
    swapped = (through == 0) & (most > 1)

    barrier = pltpu.get_barrier_semaphore()

    def greet(r, c):
        pl.semaphore_signal(barrier, inc=1, device_id=(r, c), device_id_type=MESH)

    @pl.when(z > 0)
    def _():
        greet(row, col - ACROSS)

    @pl.when(z < length - 1)
    def _():
        greet(row, col + ACROSS)

    greet(row, mate)
    for k in range(1, n_row):
        greet(lax.rem(row + k, n_row), col)

    def w_rows(r):
        size = solved.shape[0]
        return rows_w.at[pl.ds(pl.multiple_of(r * size, size), size)]

    own = [
        pltpu.make_async_copy(right, rows_r.at[:, col], own_sem.at[0]),
        pltpu.make_async_copy(left, rows_l.at[col], own_sem.at[1]),
        pltpu.make_async_copy(solved, w_rows(row), own_sem.at[2]),
        pltpu.make_async_copy(order, order_here, own_sem.at[3]),
        pltpu.make_async_copy(ranks, ranks_here, own_sem.at[4]),
    ]
    for copy in own:
        copy.start()
    pl.semaphore_wait(barrier, (z > 0).astype(jnp.int32) + (z < length - 1).astype(jnp.int32) + n_row)

    def piece(p, c):
        if p == early:
            return rows_l.at[c, pl.ds(0, cut)]
        if p == late:
            return rows_l.at[c, pl.ds(cut, cut)]
        return rows_r.at[p, c]

    def mine(p):
        if p == early:
            return left.at[pl.ds(0, cut)]
        if p == late:
            return left.at[pl.ds(cut, cut)]
        return right.at[p]

    def z_copy(p, src, way, across=False, fresh=False):
        c = src * ACROSS + ((1 - y) if across else y)
        lane = 0 if p < slots else (2 if across else 1)
        to = col + (ACROSS if way == 0 else -ACROSS)
        return pltpu.make_async_remote_copy(mine(p) if fresh else piece(p, c), piece(p, c), zsem.at[way, lane], rsem.at[p, c], device_id=(row, to), device_id_type=MESH)

    def y_copy(p, src, c, fresh=False):
        return pltpu.make_async_remote_copy(mine(p) if fresh else piece(p, c), piece(p, c), ysem.at[max(p - slots + 1, 0)], rsem.at[p, c], device_id=(row, mate), device_id_type=MESH)

    def w_copy(k):
        return pltpu.make_async_remote_copy(solved, w_rows(row), wsem.at[0], wrsem.at[0], device_id=(lax.rem(row + k, n_row), col), device_id_type=MESH)

    def upward(act):
        pl.when(z < length - 1)(functools.partial(act, 0))

    def downward(act):
        pl.when(z > 0)(functools.partial(act, 1))

    def along(side, act):
        (upward if side == 0 else downward)(act)

    def sources(d, body):
        for side in range(2):
            src = z - d if side == 0 else z + d
            ok = (src >= 0) if side == 0 else (src < length)
            pl.when(ok & (d > 0))(functools.partial(body, src, side))

    def near(d, body):
        @pl.when(d == 0)
        def _():
            body(col)

        sources(d, lambda src, side: body(src * ACROSS + y))

    def far(d, body):
        @pl.when(d == 0)
        def _():
            body(mate)

        sources(d, lambda src, side: body(src * ACROSS + 1 - y))

    where = (row, col, team, core, teams)

    def lefts(d, across, which, body):
        def one(q, _):
            last = jnp.abs(z - q)
            for s in range(1, slots):
                last = jnp.maximum(last, jnp.abs(z - q - s * half))

            @pl.when(last == d)
            def _():
                body((q * ACROSS + ((1 - y) if across else y)) * 2 + which)

            return 0

        lax.fori_loop(0, half, one, 0)

    def arrived(p, c):
        ref = piece(p, c)
        pltpu.make_async_remote_copy(ref, ref, ysem.at[0], rsem.at[p, c], device_id=(row, mate), device_id_type=MESH).wait_recv()

    for s in range(slots):
        upward(lambda way: z_copy(s, z, way, fresh=True).start())
        downward(lambda way: z_copy(s, z, way, fresh=True).start())
        y_copy(s, z, col, fresh=True).start()
    y_copy(late, z, col, fresh=True).start()
    for k in range(1, n_row):
        w_copy(k).start()

    def send_left(way):
        z_copy(early, z, way, fresh=True).start()
        z_copy(late, z, way, fresh=True).start()

    @pl.when((last_up == 0) & (z < length - 1))
    def _():
        send_left(0)

    @pl.when((last_down == 0) & (z > 0))
    def _():
        send_left(1)

    both[...] = jnp.zeros_like(both)
    for copy in own:
        copy.wait()

    root_slot = find(order_here, col)
    local = lax.rem(root_slot, slots)
    root_row = root_slot // slots
    root_team = root_row // CORES
    def pick(parts):
        value = parts[0]
        for s in range(1, slots):
            value = jnp.where(local == s, parts[s], value)
        return value

    part = depth // CORES

    def rows_of(which):
        return pl.ds(pl.multiple_of(which * part, part), part)

    def r_candidate(c, which):
        return pick([rows_r[s, c, rows_of(which)] for s in range(slots)])

    r_one, r_two, r_three, r_ready, r_drain = chain(
        where, root_row, root_team, r_candidate, lambda c, which: tile_r.at[c, rows_of(which)], ACROSS,
        rf_out, rf_in, r_chip, r_far, r_sends, rfr, rxr, rtr)

    lpart = cut // CORES

    def l_rows(u, which):
        return pl.ds(pl.multiple_of((u % 2) * cut + which * lpart, lpart), lpart)

    def l_candidate(u, which):
        return pick([rows_l[u // 2 + s * half * ACROSS, l_rows(u, which)] for s in range(slots)])

    l_one, l_two, l_three, l_ready, l_drain = chain(
        where, root_row, root_team, l_candidate, lambda u, which: tile_l.at[u // 2, l_rows(u, which)], tile_l.shape[0],
        lf_out, lf_in, l_chip, l_far, l_sends, lfr, lxr, ltr)

    r_one(col)
    r_two(col)

    held = [pltpu.make_async_copy(trailing, trail_here, held_sem.at[0]), pltpu.make_async_copy(sides_in, sides_here, held_sem.at[1])]
    for copy in held:
        copy.start()

    def relay_rights(t):
        for s in range(slots):
            def one(src, side, s=s):
                arrived(s, src * ACROSS + y)
                along(side, lambda way: z_copy(s, src, way).start())
                y_copy(s, src, src * ACROSS + y).start()

            sources(t, one)

    def own_lefts(t):
        @pl.when((t == last_up) & (z < length - 1))
        def _():
            send_left(0)

        @pl.when((t == last_down) & (z > 0))
        def _():
            send_left(1)

        @pl.when(t == 2)
        def _():
            arrived(late, mate)

        @pl.when((t == jnp.maximum(last_up, 2)) & (z < length - 1))
        def _():
            z_copy(late, z, 0, True).start()

        @pl.when((t == jnp.maximum(last_down, 2)) & (z > 0))
        def _():
            z_copy(late, z, 1, True).start()

        @pl.when(t == most)
        def _():
            y_copy(early, z, col, fresh=True).start()

    def left_arrives(k, d):
        def over(src, side):
            y_copy(early, src, src * ACROSS + y).start()

        def one(src, side):
            if k == 0:
                arrived(early, src * ACROSS + y)
                pl.when(jnp.logical_not(swapped) | (d != 1))(functools.partial(over, src, side))
                along(side, lambda way: z_copy(early, src, way).start())
            elif k == 1:
                arrived(late, src * ACROSS + y)
                along(side, lambda way: z_copy(late, src, way).start())
            elif k == 2:
                arrived(late, src * ACROSS + 1 - y)
                along(side, lambda way: z_copy(late, src, way, True).start())
            else:
                arrived(early, src * ACROSS + 1 - y)

        sources(d, one)
        if k == 0:
            pl.when(swapped & (d == 2))(lambda: sources(1, over))

    def left_unit(k, d, body):
        lefts(d, k >= 2, 1 if k in (1, 2) else 0, body)

    def w_wait():
        ref = rows_w.at[pl.ds(0, (n_row - 1) * solved.shape[0])]
        pltpu.make_async_remote_copy(ref, ref, wsem.at[0], wrsem.at[0], device_id=(row, mate), device_id_type=MESH).wait()

    def accumulate(d):
        def one(src, _):
            @pl.when(jnp.abs(z - src) == d)
            def _():
                r_ready(src)
                start = pl.multiple_of(src * (ACROSS * depth), ACROSS * depth)
                column = tile_r[pl.ds(src * ACROSS, ACROSS)].reshape(ACROSS * depth, width)
                column = cut_right(jnp.concatenate([column, rows_w[pl.ds(start, ACROSS * depth)]], axis=1), 0)
                rows = [rows_r[s, pl.ds(src * ACROSS, ACROSS)].reshape(ACROSS * depth, width) for s in range(slots)]
                both[...] += dot(cut_left(jnp.concatenate(rows, axis=1), 0), column, ((0,), (0,)))

            return 0

        lax.fori_loop(0, length, one, 0)


    def open_early():
        arrived(early, mate)
        left_arrives(3, 1)
        left_unit(3, 1, l_one)

    def other_early(d):
        @pl.when(d > 1)
        def _():
            pl.when(d == 2)(functools.partial(arrived, early, mate))
            left_arrives(3, d)
            left_unit(3, d, l_one)

    def step(t, _):
        a = jnp.where(through == 1, t - most + 1, 0)
        b = jnp.where(through == 1, 0, t - most + 1)
        c = jnp.where(through == 1, t - most + 1, jnp.where(t < 2 * most, t - most, 0))
        e = jnp.where((through == 0) & (t < 2 * most), t - most, 0)
        relay_rights(t)
        own_lefts(t)
        near(t, r_one)
        left_arrives(0, a)
        left_unit(0, a, l_one)
        left_arrives(1, a)
        left_unit(1, a, l_one)
        left_unit(0, a, l_two)
        left_arrives(2, c)
        left_unit(2, c, l_one)
        left_unit(1, a, l_two)
        near(t, r_two)
        left_arrives(0, b)
        left_unit(0, b, l_one)
        left_unit(2, c, l_two)
        other_early(e)
        left_unit(0, b, l_two)
        near(t - 1, r_three)
        far(t - 2, r_three)
        left_unit(3, jnp.where(e > 1, e, 0), l_two)
        left_arrives(1, b)
        left_unit(1, b, l_one)

        @pl.when(t == 1)
        def _():
            for s in range(slots):
                arrived(s, mate)

        def one(src, side):
            for s in range(slots):
                arrived(s, src * ACROSS + 1 - y)

        sources(t - 1, one)
        far(t - 1, r_one)
        far(t - 1, r_two)
        left_unit(1, b, l_two)

        @pl.when(t == 2)
        def _():
            w_wait()

        accumulate(jnp.where(t - 2 < most, t - 2, -1))
        return 0

    lax.fori_loop(1, jnp.maximum(2 * most + through, most + 3), step, 0)
    for copy in held:
        copy.wait()

    lane = lax.broadcasted_iota(jnp.int32, (width, mid.shape[2]), 1)
    sub = lax.broadcasted_iota(jnp.int32, (width, mid.shape[2]), 0)
    column_rank = ranks_here[col]

    def middle(s, _):
        rank = ranks_here[order_here[row * slots + s]]
        kept = (sub < rank) & ((lane < column_rank) | (lane >= width))
        mid[s] = cut_right(jnp.where(kept, both[pl.ds(pl.multiple_of(s * width, width), width)], 0.0), 0)
        return 0

    group = n_col // slots
    size = group * left.shape[0]
    own_slot = z // half

    def rows(i, _):
        b = lax.rem(own_slot + i, slots)
        here = rows_l[pl.ds(b * group, group)].reshape(size, width)
        value = dot(cut_left(here, 1), mid[b], ((1,), (0,)))
        place = pl.ds(pl.multiple_of(b * size, size), size)
        product[place] = cut_left(value[:, :width], 1)
        sides_here[place] -= value[:, width:]
        return 0

    blocks = tile_l.shape[0] // 2
    soon = (2 * z // length) * blocks
    later = blocks - soon

    def spread(u, _):
        l_three(u)
        return 0

    final = jnp.where(through == 1, 0, most)
    between = jnp.logical_not(swapped)
    pl.when(between)(open_early)
    left_arrives(2, final)
    left_unit(2, final, l_one)
    accumulate(most)
    left_unit(3, jnp.where(between, 1, 0), l_two)
    pl.when(swapped & (most == 2))(functools.partial(arrived, early, mate))
    pl.when(swapped)(lambda: left_arrives(3, 1))

    def rest(d, _):
        left_arrives(3, d)
        left_unit(3, d, l_one)
        return 0

    start = jnp.where(between, 2, most)
    lax.fori_loop(start, most + 1, rest, 0)
    lax.fori_loop(0, slots, middle, 0)
    left_unit(2, final, l_two)

    def rest_two(d, _):
        left_unit(3, d, l_two)
        return 0

    lax.fori_loop(start, most + 1, rest_two, 0)
    lax.fori_loop(0, 1, rows, 0)
    lax.fori_loop(soon * 2, (soon + blocks) * 2, spread, 0)
    lax.fori_loop(1, slots, rows, 0)
    l_ready(soon // blocks)
    wide = tile_cut.shape[0]
    tile_cut[...] = cut_right(tile_l[pl.ds(soon, blocks)].reshape(wide, width), 1)
    columns = pl.ds(pl.multiple_of(soon * left.shape[0], wide), wide)
    trail_here[:, columns] -= dot(product[...], tile_cut[...], ((1,), (1,)))
    lax.fori_loop(later * 2, (later + blocks) * 2, spread, 0)

    def leave(ref, sem):
        pltpu.make_async_remote_copy(ref, ref, sem, rsem.at[0, 0], device_id=(row, mate), device_id_type=MESH).wait_send()

    for count in range(1, length):
        for way, last in ((0, last_up), (1, last_down)):
            @pl.when(last == count - 1)
            def _(way=way, sent=count):
                leave(rows_r.at[:, pl.ds(0, sent)], zsem.at[way, 0])
                leave(rows_l.at[pl.ds(0, sent)], zsem.at[way, 1])
                leave(rows_l.at[pl.ds(0, sent), pl.ds(0, cut)], zsem.at[way, 2])

    leave(rows_r.at[:, pl.ds(0, length)], ysem.at[0])
    leave(rows_l.at[pl.ds(0, length), pl.ds(0, cut)], ysem.at[1])
    leave(rows_l.at[0, pl.ds(0, cut)], ysem.at[2])
    r_drain()
    l_drain()
    l_ready(later // blocks)


def gather(n_row, n_col, order, ranks, left, right, solved, trailing, sides_in):
    slots, depth, width = right.shape
    length = n_col // ACROSS
    teams = n_row // CORES
    f32 = jnp.float32
    lrows = left.shape[0]
    lefts = n_col // slots
    vmem = pl.BlockSpec(memory_space=pltpu.VMEM)
    hbm = pl.BlockSpec(memory_space=pltpu.HBM)
    dma = pltpu.SemaphoreType.DMA
    r_units, r_part = n_col, (depth // CORES, width)
    l_units, l_part = 2 * lefts, (lrows // 2 // CORES, width)

    def buffers(units, part):
        return [pltpu.VMEM((units,) + part, f32)] * 3 + [pltpu.VMEM((teams - 1, units) + part, f32)]

    def sems(units, group):
        return [dma((teams + 1,)), dma((units,)), dma((teams - 1, units)), dma((units // group,))]

    return pl.pallas_call(
        functools.partial(gather_kernel, n_row, n_col, slots),
        out_shape=(
            jax.ShapeDtypeStruct((n_col * lrows, 3 * width), jnp.bfloat16),
            jax.ShapeDtypeStruct((lefts,) + left.shape, f32),
            jax.ShapeDtypeStruct(trailing.shape, f32),
            jax.ShapeDtypeStruct(sides_in.shape, f32),
        ),
        in_specs=[hbm] * 7,
        out_specs=(vmem,) * 4,
        scratch_shapes=[
            pltpu.VMEM((n_col,) + left.shape, f32),
            pltpu.VMEM((slots, n_col, depth, width), f32),
            pltpu.VMEM((n_col, depth, width), f32),
            pltpu.VMEM((n_row * solved.shape[0], solved.shape[1]), f32),
            pltpu.VMEM((slots * width, width + solved.shape[1]), f32),
            pltpu.VMEM((slots, 3 * width, width + solved.shape[1]), jnp.bfloat16),
            pltpu.VMEM((lefts * lrows // 2, 3 * width), jnp.bfloat16),
            pltpu.SMEM(order.shape, order.dtype),
            pltpu.SMEM(ranks.shape, ranks.dtype),
            *buffers(r_units, r_part),
            *buffers(l_units, l_part),
            dma((5,)),
            dma((2,)),
            dma((slots + 2, n_col)),
            dma((2, 3)),
            dma((3,)),
            dma((1,)),
            dma((1,)),
            *sems(r_units, ACROSS),
            *sems(l_units, lefts),
        ],
        compiler_params=pltpu.CompilerParams(collective_id=0, has_side_effects=True, vmem_limit_bytes=GATHER_VMEM),
        name="gather_panel",
    )(*(pltpu.with_memory_space_constraint(a, pltpu.HBM) for a in (order, ranks, left, right, solved, trailing, sides_in)))


def cut_two(x):
    high = x.astype(jnp.bfloat16)
    return high, (x - high.astype(jnp.float32)).astype(jnp.bfloat16)


def cut_left(x, axis):
    high, low = cut_two(x)
    return jnp.concatenate([high, high, low], axis=axis)


def cut_right(x, axis):
    high, low = cut_two(x)
    return jnp.concatenate([high, low, high], axis=axis)


def dot(a, b, dims):
    return lax.dot_general(a, b, (dims, ((), ())), preferred_element_type=jnp.float32)


def update_kernel(length, product, tile, trailing, sides, trail_out, rhs_out, result, sems):
    rows, wide = result.shape
    blocks = 4
    size = rows // blocks
    soon = (2 * (lax.axis_index("col") // ACROSS)) // length
    here = pl.ds(pl.multiple_of(soon * wide, wide), wide)
    rest = pl.ds(pl.multiple_of((1 - soon) * wide, wide), wide)
    count = tile.shape[0] // 2
    copies = [
        pltpu.make_async_copy(trailing.at[:, here], trail_out.at[:, here], sems.at[0]),
        pltpu.make_async_copy(sides, rhs_out, sems.at[1]),
    ]
    for copy in copies:
        copy.start()
    columns = cut_right(tile[pl.ds((1 - soon) * count, count)].reshape(wide, tile.shape[2]), 1)
    for i in range(blocks):
        place = pl.ds(i * size, size)
        result[place] = trailing[place, rest] - dot(product[place], columns, ((1,), (1,)))
        copies.append(pltpu.make_async_copy(result.at[place], trail_out.at[place, rest], sems.at[2 + i]))
        copies[-1].start()
    for copy in copies:
        copy.wait()


def update(n_col, product, tile, trailing, sides):
    rows, columns = trailing.shape
    vmem = pl.BlockSpec(memory_space=pltpu.VMEM)
    hbm = pl.BlockSpec(memory_space=pltpu.HBM)
    return pl.pallas_call(
        functools.partial(update_kernel, n_col // ACROSS),
        out_shape=(jax.ShapeDtypeStruct(trailing.shape, jnp.float32), jax.ShapeDtypeStruct(sides.shape, jnp.float32)),
        in_specs=[vmem] * 4,
        out_specs=(hbm, hbm),
        scratch_shapes=[pltpu.VMEM((rows, columns // 2), jnp.float32), pltpu.SemaphoreType.DMA((6,))],
        compiler_params=pltpu.CompilerParams(vmem_limit_bytes=UPDATE_VMEM),
        name="update_panel",
    )(product, tile, trailing, sides)


def on_device(n_row, n_col, trailing, panel_left, panel_right, panel_solved, right_sides, tile_ranks, tile_order):
    parts = gather(n_row, n_col, tile_order, tile_ranks, panel_left, panel_right, panel_solved, trailing, right_sides)
    return update(n_col, *parts)


def solution(mesh):
    return jax.shard_map(
        functools.partial(on_device, mesh.shape["row"], mesh.shape["col"]),
        mesh=mesh,
        in_specs=(
            P("row", "col"),
            P(("row", "col"), None),
            P("row", "col", None),
            P("row", "col"),
            P("row", "col"),
            P(),
            P(),
        ),
        out_specs=(P("row", "col"), P("row", "col")),
        check_vma=False,
    )
```

```python
import functools

import jax
import jax.numpy as jnp
from jax import lax
from jax.experimental import pallas as pl
from jax.experimental.pallas import tpu as pltpu
from jax.sharding import PartitionSpec as P

MESH = pl.DeviceIdType.MESH
ACROSS = 2
CORES = 2
GATHER_VMEM = 30 * 1024 * 1024
UPDATE_VMEM = 16 * 1024 * 1024


def find(order, value):
    place = jnp.int32(0)
    for i in range(order.shape[0]):
        place = jnp.where(order[i] == value, jnp.int32(i), place)
    return place


def chain(where, root_row, root_team, candidate, tile_at, group, first_out, first_in, chip, far_in, sends, fr, xr, tr):
    row, col, team, core, teams = where
    pair = team * CORES + (1 - core)

    def to_pair(src, dst, sem):
        return pltpu.make_async_remote_copy(src, dst, sends.at[0], sem, device_id=(pair, col), device_id_type=MESH)

    def f_copy(u):
        return to_pair(first_out.at[u], first_in.at[u], fr.at[u])

    def x_copy(u, k):
        to = lax.rem(team + k, teams)
        return pltpu.make_async_remote_copy(chip.at[u], far_in.at[k - 1, u], sends.at[k], xr.at[k - 1, u], device_id=(to * CORES + core, col), device_id_type=MESH)

    def t_copy(u, which):
        ref = tile_at(u, which)
        return pltpu.make_async_remote_copy(ref, ref, sends.at[teams], tr.at[u // group], device_id=(pair, col), device_id_type=MESH)

    def one(u):
        first_out[u] = candidate(u, 1 - core)
        f_copy(u).start()

    def two(u):
        mine = candidate(u, core)
        f_copy(u).wait_recv()
        chip[u] = jnp.where(root_row == row, mine, first_in[u])
        for k in range(1, teams):
            x_copy(u, k).start()

    def three(u):
        value = chip[u]
        for k in range(1, teams):
            x_copy(u, k).wait_recv()
            value = jnp.where(root_team == lax.rem(team + teams - k, teams), far_in[k - 1, u], value)
        tile_at(u, core)[...] = value
        t_copy(u, core).start()

    def ready(g):
        ref = chip.at[pl.ds(g * group, group)]
        to_pair(ref, ref, tr.at[g]).wait_recv()

    def drain():
        for k in range(teams + 1):
            pltpu.make_async_remote_copy(chip, chip, sends.at[k], fr.at[0], device_id=(pair, col), device_id_type=MESH).wait_send()

    return one, two, three, ready, drain


def gather_kernel(n_row, n_col, slots, order, ranks, left, right, solved, trailing, sides_in, product, tile_l, trail_here, sides_here,
                  rows_l, rows_r, tile_r, rows_w, both, mid, tile_cut, order_here, ranks_here, rf_out, rf_in, r_chip, r_far, lf_out, lf_in, l_chip, l_far,
                  own_sem, held_sem, rsem, zsem, ysem, wsem, wrsem, r_sends, rfr, rxr, rtr, l_sends, lfr, lxr, ltr):
    length = n_col // ACROSS
    half = length // slots
    teams = n_row // CORES
    depth, width = rows_r.shape[2], rows_r.shape[3]
    cut = left.shape[0] // 2
    early, late = slots, slots + 1
    row, col = lax.axis_index("row"), lax.axis_index("col")
    z, y = col // ACROSS, col % ACROSS
    team, core = row // CORES, row % CORES
    mate = z * ACROSS + (1 - y)
    last_up, last_down = z, length - 1 - z
    most = jnp.maximum(last_up, last_down)
    through = ((z > 0) & (z < length - 1)).astype(jnp.int32)
    swapped = (through == 0) & (most > 1)

    barrier = pltpu.get_barrier_semaphore()

    def greet(r, c):
        pl.semaphore_signal(barrier, inc=1, device_id=(r, c), device_id_type=MESH)

    @pl.when(z > 0)
    def _():
        greet(row, col - ACROSS)

    @pl.when(z < length - 1)
    def _():
        greet(row, col + ACROSS)

    greet(row, mate)
    for k in range(1, n_row):
        greet(lax.rem(row + k, n_row), col)

    def w_rows(r):
        size = solved.shape[0]
        return rows_w.at[pl.ds(pl.multiple_of(r * size, size), size)]

    own = [
        pltpu.make_async_copy(right, rows_r.at[:, col], own_sem.at[0]),
        pltpu.make_async_copy(left, rows_l.at[col], own_sem.at[1]),
        pltpu.make_async_copy(solved, w_rows(row), own_sem.at[2]),
        pltpu.make_async_copy(order, order_here, own_sem.at[3]),
        pltpu.make_async_copy(ranks, ranks_here, own_sem.at[4]),
    ]
    for copy in own:
        copy.start()
    pl.semaphore_wait(barrier, (z > 0).astype(jnp.int32) + (z < length - 1).astype(jnp.int32) + n_row)

    def piece(p, c):
        if p == early:
            return rows_l.at[c, pl.ds(0, cut)]
        if p == late:
            return rows_l.at[c, pl.ds(cut, cut)]
        return rows_r.at[p, c]

    def mine(p):
        if p == early:
            return left.at[pl.ds(0, cut)]
        if p == late:
            return left.at[pl.ds(cut, cut)]
        return right.at[p]

    def z_copy(p, src, way, across=False, fresh=False):
        c = src * ACROSS + ((1 - y) if across else y)
        lane = 0 if p < slots else (2 if across else 1)
        to = col + (ACROSS if way == 0 else -ACROSS)
        return pltpu.make_async_remote_copy(mine(p) if fresh else piece(p, c), piece(p, c), zsem.at[way, lane], rsem.at[p, c], device_id=(row, to), device_id_type=MESH)

    def y_copy(p, src, c, fresh=False):
        return pltpu.make_async_remote_copy(mine(p) if fresh else piece(p, c), piece(p, c), ysem.at[max(p - slots + 1, 0)], rsem.at[p, c], device_id=(row, mate), device_id_type=MESH)

    def w_copy(k):
        return pltpu.make_async_remote_copy(solved, w_rows(row), wsem.at[0], wrsem.at[0], device_id=(lax.rem(row + k, n_row), col), device_id_type=MESH)

    def upward(act):
        pl.when(z < length - 1)(functools.partial(act, 0))

    def downward(act):
        pl.when(z > 0)(functools.partial(act, 1))

    def along(side, act):
        (upward if side == 0 else downward)(act)

    def sources(d, body):
        for side in range(2):
            src = z - d if side == 0 else z + d
            ok = (src >= 0) if side == 0 else (src < length)
            pl.when(ok & (d > 0))(functools.partial(body, src, side))

    def near(d, body):
        @pl.when(d == 0)
        def _():
            body(col)

        sources(d, lambda src, side: body(src * ACROSS + y))

    def far(d, body):
        @pl.when(d == 0)
        def _():
            body(mate)

        sources(d, lambda src, side: body(src * ACROSS + 1 - y))

    where = (row, col, team, core, teams)

    def lefts(d, across, which, body):
        def one(q, _):
            last = jnp.abs(z - q)
            for s in range(1, slots):
                last = jnp.maximum(last, jnp.abs(z - q - s * half))

            @pl.when(last == d)
            def _():
                body((q * ACROSS + ((1 - y) if across else y)) * 2 + which)

            return 0

        lax.fori_loop(0, half, one, 0)

    def arrived(p, c):
        ref = piece(p, c)
        pltpu.make_async_remote_copy(ref, ref, ysem.at[0], rsem.at[p, c], device_id=(row, mate), device_id_type=MESH).wait_recv()

    upward_first = z + 1 > length - z
    parts = 1
    small = depth // parts

    def begin(s, i, to, send_sem):
        rows = pl.ds(i * small, small)
        pltpu.make_async_remote_copy(right.at[s, rows], rows_r.at[s, col, rows], send_sem, rsem.at[s, col], device_id=(row, to), device_id_type=MESH).start()

    for s in range(slots):
        for i in range(parts):
            pl.when(upward_first & (z < length - 1))(functools.partial(begin, s, i, col + ACROSS, zsem.at[0, 0]))
            pl.when(jnp.logical_not(upward_first) & (z > 0))(functools.partial(begin, s, i, col - ACROSS, zsem.at[1, 0]))
            begin(s, i, mate, ysem.at[0])
            pl.when(jnp.logical_not(upward_first) & (z < length - 1))(functools.partial(begin, s, i, col + ACROSS, zsem.at[0, 0]))
            pl.when(upward_first & (z > 0))(functools.partial(begin, s, i, col - ACROSS, zsem.at[1, 0]))
    y_copy(late, z, col, fresh=True).start()
    for k in range(1, n_row):
        w_copy(k).start()

    def send_left(way):
        z_copy(early, z, way, fresh=True).start()
        z_copy(late, z, way, fresh=True).start()

    @pl.when((last_up == 0) & (z < length - 1))
    def _():
        send_left(0)

    @pl.when((last_down == 0) & (z > 0))
    def _():
        send_left(1)

    both[...] = jnp.zeros_like(both)
    for copy in own:
        copy.wait()

    root_slot = find(order_here, col)
    local = lax.rem(root_slot, slots)
    root_row = root_slot // slots
    root_team = root_row // CORES
    def pick(parts):
        value = parts[0]
        for s in range(1, slots):
            value = jnp.where(local == s, parts[s], value)
        return value

    part = depth // CORES

    def rows_of(which):
        return pl.ds(pl.multiple_of(which * part, part), part)

    def r_candidate(c, which):
        return pick([rows_r[s, c, rows_of(which)] for s in range(slots)])

    r_one, r_two, r_three, r_ready, r_drain = chain(
        where, root_row, root_team, r_candidate, lambda c, which: tile_r.at[c, rows_of(which)], ACROSS,
        rf_out, rf_in, r_chip, r_far, r_sends, rfr, rxr, rtr)

    lpart = cut // CORES

    def l_rows(u, which):
        return pl.ds(pl.multiple_of((u % 2) * cut + which * lpart, lpart), lpart)

    def l_candidate(u, which):
        return pick([rows_l[u // 2 + s * half * ACROSS, l_rows(u, which)] for s in range(slots)])

    l_one, l_two, l_three, l_ready, l_drain = chain(
        where, root_row, root_team, l_candidate, lambda u, which: tile_l.at[u // 2, l_rows(u, which)], tile_l.shape[0],
        lf_out, lf_in, l_chip, l_far, l_sends, lfr, lxr, ltr)

    r_one(col)
    r_two(col)

    held = [pltpu.make_async_copy(trailing, trail_here, held_sem.at[0]), pltpu.make_async_copy(sides_in, sides_here, held_sem.at[1])]
    for copy in held:
        copy.start()

    def relay_rights(t):
        for s in range(slots):
            def one(src, side, s=s):
                arrived(s, src * ACROSS + y)
                along(side, lambda way: z_copy(s, src, way).start())
                y_copy(s, src, src * ACROSS + y).start()

            sources(t, one)

    def own_lefts(t):
        @pl.when((t == last_up) & (z < length - 1))
        def _():
            send_left(0)

        @pl.when((t == last_down) & (z > 0))
        def _():
            send_left(1)

        @pl.when(t == 2)
        def _():
            arrived(late, mate)

        @pl.when((t == jnp.maximum(last_up, 2)) & (z < length - 1))
        def _():
            z_copy(late, z, 0, True).start()

        @pl.when((t == jnp.maximum(last_down, 2)) & (z > 0))
        def _():
            z_copy(late, z, 1, True).start()

        @pl.when(t == most)
        def _():
            y_copy(early, z, col, fresh=True).start()

    def left_arrives(k, d):
        def over(src, side):
            y_copy(early, src, src * ACROSS + y).start()

        def one(src, side):
            if k == 0:
                arrived(early, src * ACROSS + y)
                pl.when(jnp.logical_not(swapped) | (d != 1))(functools.partial(over, src, side))
                along(side, lambda way: z_copy(early, src, way).start())
            elif k == 1:
                arrived(late, src * ACROSS + y)
                along(side, lambda way: z_copy(late, src, way).start())
            elif k == 2:
                arrived(late, src * ACROSS + 1 - y)
                along(side, lambda way: z_copy(late, src, way, True).start())
            else:
                arrived(early, src * ACROSS + 1 - y)

        sources(d, one)
        if k == 0:
            pl.when(swapped & (d == 2))(lambda: sources(1, over))

    def left_unit(k, d, body):
        lefts(d, k >= 2, 1 if k in (1, 2) else 0, body)

    def w_wait():
        ref = rows_w.at[pl.ds(0, (n_row - 1) * solved.shape[0])]
        pltpu.make_async_remote_copy(ref, ref, wsem.at[0], wrsem.at[0], device_id=(row, mate), device_id_type=MESH).wait()

    def accumulate(d):
        def one(src, _):
            @pl.when(jnp.abs(z - src) == d)
            def _():
                r_ready(src)
                start = pl.multiple_of(src * (ACROSS * depth), ACROSS * depth)
                column = tile_r[pl.ds(src * ACROSS, ACROSS)].reshape(ACROSS * depth, width)
                column = cut_right(jnp.concatenate([column, rows_w[pl.ds(start, ACROSS * depth)]], axis=1), 0)
                rows = [rows_r[s, pl.ds(src * ACROSS, ACROSS)].reshape(ACROSS * depth, width) for s in range(slots)]
                both[...] += dot(cut_left(jnp.concatenate(rows, axis=1), 0), column, ((0,), (0,)))

            return 0

        lax.fori_loop(0, length, one, 0)


    def open_early():
        arrived(early, mate)
        left_arrives(3, 1)
        left_unit(3, 1, l_one)

    def other_early(d):
        @pl.when(d > 1)
        def _():
            pl.when(d == 2)(functools.partial(arrived, early, mate))
            left_arrives(3, d)
            left_unit(3, d, l_one)

    def step(t, _):
        a = jnp.where(through == 1, t - most + 1, 0)
        b = jnp.where(through == 1, 0, t - most + 1)
        c = jnp.where(through == 1, t - most + 1, jnp.where(t < 2 * most, t - most, 0))
        e = jnp.where((through == 0) & (t < 2 * most), t - most, 0)
        relay_rights(t)
        own_lefts(t)
        near(t, r_one)
        left_arrives(0, a)
        left_unit(0, a, l_one)
        left_arrives(1, a)
        left_unit(1, a, l_one)
        left_unit(0, a, l_two)
        left_arrives(2, c)
        left_unit(2, c, l_one)
        left_unit(1, a, l_two)
        near(t, r_two)
        left_arrives(0, b)
        left_unit(0, b, l_one)
        left_unit(2, c, l_two)
        other_early(e)
        left_unit(0, b, l_two)
        near(t - 1, r_three)
        far(t - 2, r_three)
        left_unit(3, jnp.where(e > 1, e, 0), l_two)
        left_arrives(1, b)
        left_unit(1, b, l_one)

        @pl.when(t == 1)
        def _():
            for s in range(slots):
                arrived(s, mate)

        def one(src, side):
            for s in range(slots):
                arrived(s, src * ACROSS + 1 - y)

        sources(t - 1, one)
        far(t - 1, r_one)
        far(t - 1, r_two)
        left_unit(1, b, l_two)

        @pl.when(t == 2)
        def _():
            w_wait()

        accumulate(jnp.where(t - 2 < most, t - 2, -1))
        return 0

    lax.fori_loop(1, jnp.maximum(2 * most + through, most + 3), step, 0)
    for copy in held:
        copy.wait()

    lane = lax.broadcasted_iota(jnp.int32, (width, mid.shape[2]), 1)
    sub = lax.broadcasted_iota(jnp.int32, (width, mid.shape[2]), 0)
    column_rank = ranks_here[col]

    def middle(s, _):
        rank = ranks_here[order_here[row * slots + s]]
        kept = (sub < rank) & ((lane < column_rank) | (lane >= width))
        mid[s] = cut_right(jnp.where(kept, both[pl.ds(pl.multiple_of(s * width, width), width)], 0.0), 0)
        return 0

    group = n_col // slots
    size = group * left.shape[0]
    own_slot = z // half

    def rows(i, _):
        b = lax.rem(own_slot + i, slots)
        here = rows_l[pl.ds(b * group, group)].reshape(size, width)
        value = dot(cut_left(here, 1), mid[b], ((1,), (0,)))
        place = pl.ds(pl.multiple_of(b * size, size), size)
        product[place] = cut_left(value[:, :width], 1)
        sides_here[place] -= value[:, width:]
        return 0

    blocks = tile_l.shape[0] // 2
    soon = (2 * z // length) * blocks
    later = blocks - soon

    def spread(u, _):
        l_three(u)
        return 0

    final = jnp.where(through == 1, 0, most)
    between = jnp.logical_not(swapped)
    pl.when(between)(open_early)
    left_arrives(2, final)
    left_unit(2, final, l_one)
    accumulate(most)
    left_unit(3, jnp.where(between, 1, 0), l_two)
    pl.when(swapped & (most == 2))(functools.partial(arrived, early, mate))
    pl.when(swapped)(lambda: left_arrives(3, 1))

    def rest(d, _):
        left_arrives(3, d)
        left_unit(3, d, l_one)
        return 0

    start = jnp.where(between, 2, most)
    lax.fori_loop(start, most + 1, rest, 0)
    lax.fori_loop(0, slots, middle, 0)
    left_unit(2, final, l_two)

    def rest_two(d, _):
        left_unit(3, d, l_two)
        return 0

    lax.fori_loop(start, most + 1, rest_two, 0)
    lax.fori_loop(0, 1, rows, 0)
    lax.fori_loop(soon * 2, (soon + blocks) * 2, spread, 0)
    lax.fori_loop(1, slots, rows, 0)
    l_ready(soon // blocks)
    wide = tile_cut.shape[0]
    tile_cut[...] = cut_right(tile_l[pl.ds(soon, blocks)].reshape(wide, width), 1)
    columns = pl.ds(pl.multiple_of(soon * left.shape[0], wide), wide)
    trail_here[:, columns] -= dot(product[...], tile_cut[...], ((1,), (1,)))
    lax.fori_loop(later * 2, (later + blocks) * 2, spread, 0)

    def leave(ref, sem):
        pltpu.make_async_remote_copy(ref, ref, sem, rsem.at[0, 0], device_id=(row, mate), device_id_type=MESH).wait_send()

    for count in range(1, length):
        for way, last in ((0, last_up), (1, last_down)):
            @pl.when(last == count - 1)
            def _(way=way, sent=count):
                leave(rows_r.at[:, pl.ds(0, sent)], zsem.at[way, 0])
                leave(rows_l.at[pl.ds(0, sent)], zsem.at[way, 1])
                leave(rows_l.at[pl.ds(0, sent), pl.ds(0, cut)], zsem.at[way, 2])

    leave(rows_r.at[:, pl.ds(0, length)], ysem.at[0])
    leave(rows_l.at[pl.ds(0, length), pl.ds(0, cut)], ysem.at[1])
    leave(rows_l.at[0, pl.ds(0, cut)], ysem.at[2])
    r_drain()
    l_drain()
    l_ready(later // blocks)


def gather(n_row, n_col, order, ranks, left, right, solved, trailing, sides_in):
    slots, depth, width = right.shape
    length = n_col // ACROSS
    teams = n_row // CORES
    f32 = jnp.float32
    lrows = left.shape[0]
    lefts = n_col // slots
    vmem = pl.BlockSpec(memory_space=pltpu.VMEM)
    hbm = pl.BlockSpec(memory_space=pltpu.HBM)
    dma = pltpu.SemaphoreType.DMA
    r_units, r_part = n_col, (depth // CORES, width)
    l_units, l_part = 2 * lefts, (lrows // 2 // CORES, width)

    def buffers(units, part):
        return [pltpu.VMEM((units,) + part, f32)] * 3 + [pltpu.VMEM((teams - 1, units) + part, f32)]

    def sems(units, group):
        return [dma((teams + 1,)), dma((units,)), dma((teams - 1, units)), dma((units // group,))]

    return pl.pallas_call(
        functools.partial(gather_kernel, n_row, n_col, slots),
        out_shape=(
            jax.ShapeDtypeStruct((n_col * lrows, 3 * width), jnp.bfloat16),
            jax.ShapeDtypeStruct((lefts,) + left.shape, f32),
            jax.ShapeDtypeStruct(trailing.shape, f32),
            jax.ShapeDtypeStruct(sides_in.shape, f32),
        ),
        in_specs=[hbm] * 7,
        out_specs=(vmem,) * 4,
        scratch_shapes=[
            pltpu.VMEM((n_col,) + left.shape, f32),
            pltpu.VMEM((slots, n_col, depth, width), f32),
            pltpu.VMEM((n_col, depth, width), f32),
            pltpu.VMEM((n_row * solved.shape[0], solved.shape[1]), f32),
            pltpu.VMEM((slots * width, width + solved.shape[1]), f32),
            pltpu.VMEM((slots, 3 * width, width + solved.shape[1]), jnp.bfloat16),
            pltpu.VMEM((lefts * lrows // 2, 3 * width), jnp.bfloat16),
            pltpu.SMEM(order.shape, order.dtype),
            pltpu.SMEM(ranks.shape, ranks.dtype),
            *buffers(r_units, r_part),
            *buffers(l_units, l_part),
            dma((5,)),
            dma((2,)),
            dma((slots + 2, n_col)),
            dma((2, 3)),
            dma((3,)),
            dma((1,)),
            dma((1,)),
            *sems(r_units, ACROSS),
            *sems(l_units, lefts),
        ],
        compiler_params=pltpu.CompilerParams(collective_id=0, has_side_effects=True, vmem_limit_bytes=GATHER_VMEM),
        name="gather_panel",
    )(*(pltpu.with_memory_space_constraint(a, pltpu.HBM) for a in (order, ranks, left, right, solved, trailing, sides_in)))


def cut_two(x):
    high = x.astype(jnp.bfloat16)
    return high, (x - high.astype(jnp.float32)).astype(jnp.bfloat16)


def cut_left(x, axis):
    high, low = cut_two(x)
    return jnp.concatenate([high, high, low], axis=axis)


def cut_right(x, axis):
    high, low = cut_two(x)
    return jnp.concatenate([high, low, high], axis=axis)


def dot(a, b, dims):
    return lax.dot_general(a, b, (dims, ((), ())), preferred_element_type=jnp.float32)


def update_kernel(length, product, tile, trailing, sides, trail_out, rhs_out, result, sems):
    rows, wide = result.shape
    blocks = 4
    size = rows // blocks
    soon = (2 * (lax.axis_index("col") // ACROSS)) // length
    here = pl.ds(pl.multiple_of(soon * wide, wide), wide)
    rest = pl.ds(pl.multiple_of((1 - soon) * wide, wide), wide)
    count = tile.shape[0] // 2
    copies = [
        pltpu.make_async_copy(trailing.at[:, here], trail_out.at[:, here], sems.at[0]),
        pltpu.make_async_copy(sides, rhs_out, sems.at[1]),
    ]
    for copy in copies:
        copy.start()
    columns = cut_right(tile[pl.ds((1 - soon) * count, count)].reshape(wide, tile.shape[2]), 1)
    for i in range(blocks):
        place = pl.ds(i * size, size)
        result[place] = trailing[place, rest] - dot(product[place], columns, ((1,), (1,)))
        copies.append(pltpu.make_async_copy(result.at[place], trail_out.at[place, rest], sems.at[2 + i]))
        copies[-1].start()
    for copy in copies:
        copy.wait()


def update(n_col, product, tile, trailing, sides):
    rows, columns = trailing.shape
    vmem = pl.BlockSpec(memory_space=pltpu.VMEM)
    hbm = pl.BlockSpec(memory_space=pltpu.HBM)
    return pl.pallas_call(
        functools.partial(update_kernel, n_col // ACROSS),
        out_shape=(jax.ShapeDtypeStruct(trailing.shape, jnp.float32), jax.ShapeDtypeStruct(sides.shape, jnp.float32)),
        in_specs=[vmem] * 4,
        out_specs=(hbm, hbm),
        scratch_shapes=[pltpu.VMEM((rows, columns // 2), jnp.float32), pltpu.SemaphoreType.DMA((6,))],
        compiler_params=pltpu.CompilerParams(vmem_limit_bytes=UPDATE_VMEM),
        name="update_panel",
    )(product, tile, trailing, sides)


def on_device(n_row, n_col, trailing, panel_left, panel_right, panel_solved, right_sides, tile_ranks, tile_order):
    parts = gather(n_row, n_col, tile_order, tile_ranks, panel_left, panel_right, panel_solved, trailing, right_sides)
    return update(n_col, *parts)


def solution(mesh):
    return jax.shard_map(
        functools.partial(on_device, mesh.shape["row"], mesh.shape["col"]),
        mesh=mesh,
        in_specs=(
            P("row", "col"),
            P(("row", "col"), None),
            P("row", "col", None),
            P("row", "col"),
            P("row", "col"),
            P(),
            P(),
        ),
        out_specs=(P("row", "col"), P("row", "col")),
        check_vma=False,
    )
```
